512 devices in a mesh: seq: 64 (over y, x, core), tp: 8 (over z).
Axes of the slice: x: 4, y: 8, z: 8, core: 2. Of those that a mesh axis runs over, the one named last changes fastest.
Arguments:
- query: bfloat16 [512, 2048], P('seq', 'tp'), may hold values from -8 to 8, as said below
- new_key: bfloat16 [512, 2048], P('seq', 'tp'), may hold values from -6 to 6
- new_value: bfloat16 [512, 2048], P('seq', 'tp'), may hold values from -6 to 6
- key_pool: bfloat16 [2560, 64, 2048], P('seq', None, 'tp'), may hold values from -6 to 6
- value_pool: bfloat16 [2560, 64, 2048], P('seq', None, 'tp'), may hold values from -6 to 6
- long_key: bfloat16 [4, 16384, 2048], P(None, 'seq', 'tp'), may hold values from -6 to 6
- long_value: bfloat16 [4, 16384, 2048], P(None, 'seq', 'tp'), may hold values from -6 to 6
- serve_table: int32 [640], P('seq'), may hold values from -1 to 511, as said below
- serve_len: int32 [640], P('seq'), may hold values from 0 to 256, as said below
- page_slot: int32 [2560], P('seq'), may hold values from -1 to 9, as said below
- page_offset: int32 [2560], P('seq'), may hold values from 0 to 192, as said below
- long_request: int32 [4], replicated, may hold values from 7 to 511, as said below
- long_len: int32 [4], replicated, may hold values from 8192 to 16384
- lambda_head: float32 [8], P('tp'), may hold values from 0.2 to 0.8
- norm_gain: float32 [2048], P('tp'), may hold values from 0.5 to 1.5
- out_weight: bfloat16 [2048, 2048], P('tp'), may hold values from -0.125 to 0.125
Outputs:
- layer_out: bfloat16 [512, 2048], P('seq', 'tp')
The draws below stay inside these ranges and needn't reach their ends.
Inputs may be any that keep to these rules, and one draw needn't show every extreme that they name: `query`: rows r with r % 4 == 0 or r % 8 == 7 and all others follow the table's range. `serve_table`: every request that is not a long request stands in exactly one slot, possibly of another index of seq than its own; long requests stand in none; some index of seq fills all 10 slots. `serve_len`: the length of a request that stands in a slot is 1 or more. `page_slot`: A slot of length L owns exactly ceil(L / 64) pages of its own index of seq, with offsets 0, 64, 128 and so on; some index of seq uses all 40 pages. `page_offset`: free pages have offset 0. `long_request`: distinct request numbers.
All inputs are finite; a program needn't handle non-finite values.
Results may differ from the reference program's by a relative error of at most 0.019.
Values may be sent and summed in bfloat16 or wider, within the bound.
No kernel may reach another device: no remote copies, remote signals or barrier semaphores. Data moves between devices by JAX's collectives and lax.ppermute only.
A program may use at most 64 MiB of HBM per device.

```python
import jax
import jax.numpy as jnp
from jax import lax

D = 2048
HEADS = 8
DH = 128
DV = 256
REQ_DEV = 8
PG = 64
MAXP = 4
NLONG = 4
LLEN_DEV = 256
SERVE = 10
PAGES_DEV = 40
REQS = 512
POOL = 2560
LLEN = 16384
N_SEQ = 64


def layout(key):
    layout_key = jax.random.fold_in(key, 7001)
    n_devices = REQS // REQ_DEV
    stride = n_devices // NLONG
    long_index = jnp.arange(NLONG)
    jitter = jax.random.randint(jax.random.fold_in(layout_key, 10), (NLONG,), 0, max(stride // 2, 1))
    jitter = jnp.where((long_index == 0) | (long_index == NLONG - 1), 0, jitter)
    long_dev = jnp.where(long_index == NLONG - 1, 0, n_devices - 1 - long_index * stride - 2 * jitter)
    start_dev = n_devices - 2 - jax.random.randint(jax.random.fold_in(layout_key, 1), (), 0, NLONG - 1) * stride
    offset_dev = jax.random.randint(jax.random.fold_in(layout_key, 2), (), 1, n_devices)
    devices = jnp.arange(n_devices)
    leaving = jax.random.randint(jax.random.fold_in(layout_key, 3), (n_devices,), 0, 3)
    sender = (start_dev - offset_dev) % n_devices
    leaving = jnp.where(devices == start_dev, 0, leaving)
    leaving = jnp.where(devices == sender, 2, leaving)
    long_ids = long_dev * REQ_DEV + REQ_DEV - 1
    is_long_dev = jnp.any(devices[:, None] == long_dev[None, :], axis=1)
    requests = jnp.arange(REQS)
    home_dev = requests // REQ_DEV
    local_idx = requests % REQ_DEV
    lengths = jax.random.randint(jax.random.fold_in(layout_key, 4), (REQS,), PG // 2, MAXP * PG + 1)
    full_len = jax.random.randint(jax.random.fold_in(layout_key, 5), (REQS,), (MAXP - 1) * PG + 1, MAXP * PG + 1)
    forced = (home_dev == start_dev) | (home_dev == sender) & (local_idx < 2)
    lengths = jnp.where(forced, full_len, lengths)
    lengths = jnp.where(requests == start_dev * REQ_DEV, MAXP * PG, lengths)
    own_slots = jnp.arange(REQ_DEV)
    own_ids = devices[:, None] * REQ_DEV + own_slots[None, :]
    own_ok = (own_slots[None, :] >= leaving[:, None]) & jnp.logical_not((own_slots[None, :] == REQ_DEV - 1) & is_long_dev[:, None])
    source = (devices - offset_dev) % n_devices
    in_slots = jnp.arange(2)
    in_ids = source[:, None] * REQ_DEV + in_slots[None, :]
    in_ok = in_slots[None, :] < leaving[source][:, None]
    serve_ids = jnp.concatenate([jnp.where(own_ok, own_ids, -1), jnp.where(in_ok, in_ids, -1)], axis=1)
    slot_len = jnp.where(serve_ids >= 0, lengths[jnp.maximum(serve_ids, 0)], 0)
    counts = (slot_len + PG - 1) // PG
    first_page = jnp.cumsum(counts, axis=1) - counts
    page_ids = jnp.arange(PAGES_DEV)
    inside = (page_ids[None, None, :] >= first_page[:, :, None]) & (page_ids[None, None, :] < (first_page + counts)[:, :, None])
    slot_of = jnp.sum(jnp.where(inside, jnp.arange(SERVE)[None, :, None] + 1, 0), axis=1) - 1
    page_off = jnp.sum(jnp.where(inside, (page_ids[None, None, :] - first_page[:, :, None]) * PG, 0), axis=1)
    perm_key = jax.random.fold_in(layout_key, 6)
    orders = jax.vmap(lambda device: jax.random.permutation(jax.random.fold_in(perm_key, device), PAGES_DEV))(devices)
    slot_of = jnp.take_along_axis(slot_of, orders, axis=1)
    page_off = jnp.take_along_axis(page_off, orders, axis=1)
    long_order = jax.random.permutation(jax.random.fold_in(layout_key, 11), NLONG)
    long_ids = long_ids[long_order]
    longest = jax.random.randint(jax.random.fold_in(layout_key, 8), (), 0, NLONG)
    long_lengths = jax.random.randint(jax.random.fold_in(layout_key, 9), (NLONG,), LLEN // 2, LLEN + 1)
    long_lengths = jnp.where(jnp.arange(NLONG) == longest, LLEN, long_lengths)
    return (serve_ids, slot_len, slot_of, page_off, long_ids, long_lengths)


def draw_serve_table(key, part):
    return layout(key)[0].reshape(-1).astype(jnp.int32)


def draw_serve_len(key, part):
    return layout(key)[1].reshape(-1).astype(jnp.int32)


def draw_page_slot(key, part):
    return layout(key)[2].reshape(-1).astype(jnp.int32)


def draw_page_offset(key, part):
    return layout(key)[3].reshape(-1).astype(jnp.int32)


def draw_long_request(key, part):
    return layout(key)[4].astype(jnp.int32)


def draw_long_len(key, part):
    return layout(key)[5].astype(jnp.int32)


def draw_query(key, part):
    shape = (REQS, HEADS * 2 * DH)
    values = jnp.clip(jax.random.normal(jax.random.fold_in(key, 9201), shape, jnp.float32), -6.0, 6.0)
    return values.astype(jnp.bfloat16)


def draw_key_pool(key, part):
    shape = (POOL, PG, HEADS * 2 * DH)
    values = jnp.clip(jax.random.normal(jax.random.fold_in(key, 9301), shape, jnp.float32), -6.0, 6.0)
    return values.astype(jnp.bfloat16)


def draw_long_key(key, part):
    shape = (NLONG, LLEN, HEADS * 2 * DH)
    values = jnp.clip(jax.random.normal(jax.random.fold_in(key, 9401), shape, jnp.float32), -6.0, 6.0)
    return values.astype(jnp.bfloat16)


def steps_of(rng, shape, split, low, top_value):
    level, own = 1.0, jax.random.fold_in(rng, 6)
    for axis_at, shards_of in split:
        steps = jnp.exp(jax.random.uniform(jax.random.fold_in(own, axis_at), (shards_of,), jnp.float32, low / len(split), top_value / len(split)))
        level = level * jnp.repeat(steps, shape[axis_at] // shards_of).reshape([-1 if axis == axis_at else 1 for axis in range(len(shape))])
    return level


def gaussian(stream_key, shape, scale, reach, cuts=(), kind=jnp.bfloat16):
    values = scale * jax.random.normal(stream_key, shape, jnp.float32)
    if cuts:
        values = values * steps_of(stream_key, shape, cuts, -0.22, 0.18)
    return jnp.clip(values, -reach, reach).astype(kind)


def setup_inputs(seed: int = 0) -> dict:
    key_of = jax.random.split(jax.random.key(seed), 17)
    return {
        "query": draw_query(jax.random.fold_in(key_of[16], 71), 0),
        "new_key": gaussian(key_of[1], (REQS, HEADS * 2 * DH), 1.0, 6.0, ((0, 64), (1, 8))),
        "new_value": gaussian(key_of[2], (REQS, HEADS * DV), 1.0, 6.0, ((0, 64), (1, 8))),
        "key_pool": draw_key_pool(jax.random.fold_in(key_of[16], 71), 0),
        "value_pool": gaussian(key_of[4], (POOL, PG, HEADS * DV), 1.0, 6.0, ((0, 64), (2, 8))),
        "long_key": draw_long_key(jax.random.fold_in(key_of[16], 71), 0),
        "long_value": gaussian(key_of[6], (NLONG, LLEN, HEADS * DV), 1.0, 6.0, ((1, 64), (2, 8))),
        "serve_table": draw_serve_table(jax.random.fold_in(key_of[16], 71), 0),
        "serve_len": draw_serve_len(jax.random.fold_in(key_of[16], 71), 0),
        "page_slot": draw_page_slot(jax.random.fold_in(key_of[16], 71), 0),
        "page_offset": draw_page_offset(jax.random.fold_in(key_of[16], 71), 0),
        "long_request": draw_long_request(jax.random.fold_in(key_of[16], 71), 0),
        "long_len": draw_long_len(jax.random.fold_in(key_of[16], 71), 0),
        "lambda_head": jnp.clip(0.2 + 0.6 * jax.random.uniform(key_of[13], (HEADS,), jnp.float32) ** steps_of(key_of[13], (HEADS,), ((0, 8),), -0.2, 0.2), 0.2, 0.8),
        "norm_gain": jnp.clip(1.0 + 0.1 * jax.random.normal(key_of[14], (HEADS * DV,), jnp.float32), 0.5, 1.5),
        "out_weight": gaussian(key_of[15], (HEADS * DV, D), (HEADS * DV) ** -0.5, 0.125, ((0, 8),)),
    }


MASKED = -1e+30

def page_terms(keys, values, page_q, live):
    page_count = keys.shape[0]
    cell_count = keys.shape[1]
    head_count = page_q.shape[1]
    shaped_keys = keys.astype(jnp.float32).reshape(page_count, cell_count, head_count, 2, DH)
    scores = jnp.einsum('pchjd,phjd->pchj', shaped_keys, page_q.astype(jnp.float32), precision=lax.Precision.HIGHEST) * DH ** (-0.5)
    live_mask = live[:, :, None, None]
    scores = jnp.where(live_mask, scores, MASKED)
    page_max = lax.optimization_barrier(jnp.max(scores, axis=1))
    weights = jnp.where(live_mask, jnp.exp(scores - page_max[:, None]), 0.0)
    page_sum = lax.optimization_barrier(jnp.sum(weights, axis=1))
    rounded = lax.optimization_barrier(weights.astype(jnp.bfloat16)).astype(jnp.float32)
    shaped_values = values.astype(jnp.float32).reshape(page_count, cell_count, head_count, DV)
    page_num = jnp.einsum('pchj,pchv->phjv', rounded, shaped_values, precision=lax.Precision.HIGHEST)
    return (page_max, page_sum, page_num)

def block_terms(operands):
    return page_terms(operands[0], operands[1], operands[2], operands[3])

def reference(query, new_key, new_value, key_pool, value_pool, long_key, long_value, serve_table, serve_len, page_slot, page_offset, long_request, long_len, lambda_head, norm_gain, out_weight):
    queries = query.reshape(REQS, HEADS, 2, DH)
    device_of = jnp.arange(POOL, dtype=jnp.int32) // PAGES_DEV
    slot_index = (device_of * SERVE + jnp.maximum(page_slot, 0)).astype(jnp.int32)
    page_req = jnp.where(page_slot >= 0, serve_table[slot_index], -1)
    page_len = jnp.where(page_slot >= 0, serve_len[slot_index], 0)
    page_q = queries[jnp.maximum(page_req, 0)]
    cell_pos = page_offset[:, None] + jnp.arange(PG, dtype=jnp.int32)[None, :]
    live = (page_slot[:, None] >= 0) & (cell_pos < page_len[:, None])
    pool_max, pool_sum, pool_num = lax.map(block_terms, (key_pool.reshape(N_SEQ, PAGES_DEV, PG, HEADS * 2 * DH), value_pool.reshape(N_SEQ, PAGES_DEV, PG, HEADS * DV), page_q.reshape(N_SEQ, PAGES_DEV, HEADS, 2, DH), live.reshape(N_SEQ, PAGES_DEV, PG)))
    pool_max = pool_max.reshape(POOL, HEADS, 2)
    pool_sum = pool_sum.reshape(POOL, HEADS, 2)
    pool_num = pool_num.reshape(POOL, HEADS, 2, DV)
    per_long = LLEN // PG
    long_pages = NLONG * per_long
    long_q = jnp.repeat(queries[long_request], per_long, axis=0)
    long_pos = jnp.arange(LLEN, dtype=jnp.int32).reshape(per_long, PG)
    long_live = (long_pos[None] < long_len[:, None, None]).reshape(long_pages, PG)
    block_pages = LLEN_DEV // PG
    long_max, long_sum, long_num = lax.map(block_terms, (long_key.reshape(NLONG * N_SEQ, block_pages, PG, HEADS * 2 * DH), long_value.reshape(NLONG * N_SEQ, block_pages, PG, HEADS * DV), long_q.reshape(NLONG * N_SEQ, block_pages, HEADS, 2, DH), long_live.reshape(NLONG * N_SEQ, block_pages, PG)))
    every_max = jnp.concatenate([pool_max, long_max.reshape(long_pages, HEADS, 2)], axis=0)
    every_sum = jnp.concatenate([pool_sum, long_sum.reshape(long_pages, HEADS, 2)], axis=0)
    every_num = jnp.concatenate([pool_num, long_num.reshape(long_pages, HEADS, 2, DV)], axis=0)
    owner_ids = jnp.concatenate([page_req, jnp.repeat(long_request, per_long)], axis=0).astype(jnp.int32)
    segment = jnp.where(owner_ids >= 0, owner_ids, REQS).astype(jnp.int32)
    own_scores = jnp.einsum('rhjd,rhjd->rhj', queries.astype(jnp.float32), new_key.reshape(REQS, HEADS, 2, DH).astype(jnp.float32), precision=lax.Precision.HIGHEST) * DH ** (-0.5)
    seg_max = jax.ops.segment_max(every_max, segment, num_segments=REQS + 1)[:REQS]
    best = jnp.maximum(own_scores, seg_max)
    best_ext = jnp.concatenate([best, jnp.zeros((1, HEADS, 2), jnp.float32)], axis=0)
    valid = (owner_ids >= 0)[:, None, None]
    factor = jnp.where(valid, jnp.exp(jnp.where(valid, every_max - best_ext[segment], 0.0)), 0.0)
    own_weight = jnp.exp(own_scores - best)
    denom = own_weight + jax.ops.segment_sum(factor * every_sum, segment, num_segments=REQS + 1)[:REQS]
    numer = own_weight[..., None] * new_value.reshape(REQS, HEADS, 1, DV).astype(jnp.float32)
    numer = numer + jax.ops.segment_sum(factor[..., None] * every_num, segment, num_segments=REQS + 1)[:REQS]
    attn = numer / denom[..., None]
    diff = attn[:, :, 0] - lambda_head[None, :, None] * attn[:, :, 1]
    normed = diff * lax.rsqrt(lax.optimization_barrier(jnp.mean(diff * diff, axis=-1, keepdims=True)) + 1e-05) * norm_gain.reshape(HEADS, DV)
    normed = normed.astype(jnp.bfloat16).reshape(REQS, HEADS * DV)
    return jnp.dot(normed, out_weight, preferred_element_type=jnp.float32).astype(jnp.bfloat16)
```

```python
import jax
import jax.numpy as jnp
from jax import lax
from jax.sharding import PartitionSpec as P

DH = 128
DV = 256
PG = 64


MASKED = -1e30


def page_terms(keys, values, page_q, live):
    page_count = keys.shape[0]
    cell_count = keys.shape[1]
    shaped_keys = keys.reshape(page_count, cell_count, 2, DH)
    scores = jnp.einsum(
        "pcjd,pjd->pcj", shaped_keys, page_q, preferred_element_type=jnp.float32
    ) * DH ** (-0.5)
    live_mask = live[:, :, None]
    scores = jnp.where(live_mask, scores, MASKED)
    page_max = jnp.max(scores, axis=1)
    weights = jnp.where(live_mask, jnp.exp(scores - page_max[:, None]), 0.0)
    page_sum = jnp.sum(weights, axis=1)
    page_num = jnp.einsum(
        "pcj,pcv->pjv",
        weights.astype(jnp.bfloat16),
        values,
        preferred_element_type=jnp.float32,
    )
    return (page_max, page_sum, page_num)


def fold_pages(page_max, page_sum, page_num, owners, group_count):
    member = (owners[:, None] == jnp.arange(group_count)[None, :])[:, :, None]
    group_max = jnp.max(jnp.where(member, page_max[:, None], MASKED), axis=0)
    factor = jnp.where(
        member, jnp.exp(jnp.where(member, page_max[:, None] - group_max[None], 0.0)), 0.0
    )
    group_sum = jnp.einsum("pgj,pj->gj", factor, page_sum, precision=lax.Precision.HIGHEST)
    group_num = jnp.einsum("pgj,pjv->gjv", factor, page_num, precision=lax.Precision.HIGHEST)
    return (group_max, group_sum, group_num)


def on_device(
    query,
    new_key,
    new_value,
    key_pool,
    value_pool,
    long_key,
    long_value,
    serve_table,
    serve_len,
    page_slot,
    page_offset,
    long_request,
    long_len,
    lambda_head,
    norm_gain,
    out_weight,
):
    req_count = query.shape[0]
    serve_count = serve_table.shape[0]
    long_count = long_request.shape[0]
    seq_index = lax.axis_index("seq")
    seq_count = lax.axis_size("seq")
    tp_count = lax.axis_size("tp")
    all_queries = lax.all_to_all(
        jnp.broadcast_to(query[None], (seq_count,) + query.shape), "seq", 0, 0, tiled=True
    ).reshape(-1, 2, DH)
    slot_queries = all_queries[jnp.maximum(serve_table, 0)]
    safe_slot = jnp.maximum(page_slot, 0)
    cell_pos = page_offset[:, None] + jnp.arange(key_pool.shape[1])[None, :]
    live = (page_slot[:, None] >= 0) & (cell_pos < serve_len[safe_slot][:, None])
    pool_max, pool_sum, pool_num = page_terms(key_pool, value_pool, slot_queries[safe_slot], live)
    slot_max, slot_sum, slot_num = fold_pages(pool_max, pool_sum, pool_num, page_slot, serve_count)
    long_cells = long_key.shape[1]
    per_long = long_cells // PG
    long_pages = long_count * per_long
    long_queries = jnp.repeat(all_queries[long_request], per_long, axis=0)
    long_pos = seq_index * long_cells + jnp.arange(long_cells)
    long_live = (long_pos[None, :] < long_len[:, None]).reshape(long_pages, PG)
    part_max, part_sum, part_num = page_terms(
        long_key.reshape(long_pages, PG, -1),
        long_value.reshape(long_pages, PG, -1),
        long_queries,
        long_live,
    )
    long_owner = jnp.repeat(jnp.arange(long_count), per_long)
    long_max, long_sum, long_num = fold_pages(part_max, part_sum, part_num, long_owner, long_count)
    row_max = jnp.concatenate([slot_max, long_max], axis=0)
    row_sum = jnp.concatenate([slot_sum, long_sum], axis=0)
    row_num = jnp.concatenate([slot_num, long_num], axis=0)
    row_req = jnp.concatenate([serve_table, long_request], axis=0)
    row_count = row_req.shape[0]
    width = 2 * DV + 8
    packed = jnp.concatenate(
        [
            row_num.reshape(row_count, 2 * DV),
            row_max,
            row_sum,
            jnp.zeros((row_count, width - 2 * DV - 4), jnp.float32),
        ],
        axis=1,
    )
    empty = jnp.concatenate(
        [
            jnp.zeros((1, 2 * DV), jnp.float32),
            jnp.full((1, 2), MASKED, jnp.float32),
            jnp.zeros((1, width - 2 * DV - 2), jnp.float32),
        ],
        axis=1,
    )
    total = seq_count * req_count
    target = jnp.where(row_req >= 0, row_req, total)
    outbox = jnp.broadcast_to(empty, (total + 1, width)).at[target].set(packed)[:total]
    inbox = lax.all_to_all(
        outbox.reshape(seq_count, 1, req_count * width), "seq", 0, 0, tiled=True
    ).reshape(seq_count, req_count, width)
    in_num = inbox[:, :, : 2 * DV].reshape(seq_count, req_count, 2, DV)
    in_max = inbox[:, :, 2 * DV : 2 * DV + 2]
    in_sum = inbox[:, :, 2 * DV + 2 : 2 * DV + 4]
    own_queries = query.reshape(req_count, 2, DH)
    own_keys = new_key.reshape(req_count, 2, DH)
    own_scores = jnp.einsum(
        "rjd,rjd->rj", own_queries, own_keys, preferred_element_type=jnp.float32
    ) * DH ** (-0.5)
    best = jnp.maximum(own_scores, jnp.max(in_max, axis=0))
    factor = jnp.exp(in_max - best[None])
    own_weight = jnp.exp(own_scores - best)
    denom = own_weight + jnp.sum(factor * in_sum, axis=0)
    numer = own_weight[..., None] * new_value.reshape(req_count, 1, DV).astype(jnp.float32)
    numer = numer + jnp.sum(factor[..., None] * in_num, axis=0)
    attn = numer / denom[..., None]
    diff = attn[:, 0] - lambda_head[0] * attn[:, 1]
    normed = (
        diff
        * lax.rsqrt(jnp.mean(diff * diff, axis=-1, keepdims=True) + 1e-05)
        * norm_gain.reshape(1, DV)
    )
    normed = normed.astype(jnp.bfloat16)
    partial_out = jnp.dot(normed, out_weight, preferred_element_type=jnp.float32)
    cols = partial_out.shape[1] // tp_count
    pieces = lax.all_to_all(
        partial_out.reshape(req_count, tp_count, cols).transpose(1, 0, 2), "tp", 0, 0, tiled=True
    )
    return jnp.sum(pieces, axis=0).astype(jnp.bfloat16)


def solution(mesh):
    return jax.shard_map(
        on_device,
        mesh=mesh,
        in_specs=(
            P("seq", "tp"),
            P("seq", "tp"),
            P("seq", "tp"),
            P("seq", None, "tp"),
            P("seq", None, "tp"),
            P(None, "seq", "tp"),
            P(None, "seq", "tp"),
            P("seq"),
            P("seq"),
            P("seq"),
            P("seq"),
            P(),
            P(),
            P("tp"),
            P("tp"),
            P("tp", None),
        ),
        out_specs=P("seq", "tp"),
        check_vma=False,
    )
```

```python
import jax
import jax.numpy as jnp
from jax import lax
from jax.sharding import PartitionSpec as P

DH = 128
DV = 256
PG = 64


MASKED = -1e30


def page_terms(keys, values, page_q, live):
    page_count = keys.shape[0]
    cell_count = keys.shape[1]
    shaped_keys = keys.reshape(page_count, cell_count, 2, DH)
    scores = jnp.einsum(
        "pcjd,pjd->pcj", shaped_keys, page_q, preferred_element_type=jnp.float32
    ) * DH ** (-0.5)
    live_mask = live[:, :, None]
    scores = jnp.where(live_mask, scores, MASKED)
    page_max = jnp.max(scores, axis=1)
    weights = jnp.where(live_mask, jnp.exp(scores - page_max[:, None]), 0.0)
    page_sum = jnp.sum(weights, axis=1)
    page_num = jnp.einsum(
        "pcj,pcv->pjv",
        weights.astype(jnp.bfloat16),
        values,
        preferred_element_type=jnp.float32,
    )
    return (page_max, page_sum, page_num)


def fold_pages(page_max, page_sum, page_num, owners, group_count):
    member = (owners[:, None] == jnp.arange(group_count)[None, :])[:, :, None]
    group_max = jnp.max(jnp.where(member, page_max[:, None], MASKED), axis=0)
    factor = jnp.where(
        member, jnp.exp(jnp.where(member, page_max[:, None] - group_max[None], 0.0)), 0.0
    )
    group_sum = jnp.einsum("pgj,pj->gj", factor, page_sum, precision=lax.Precision.HIGHEST)
    group_num = jnp.einsum("pgj,pjv->gjv", factor, page_num, precision=lax.Precision.HIGHEST)
    return (group_max, group_sum, group_num)


def split_three(x):
    hi = lax.reduce_precision(x, exponent_bits=8, mantissa_bits=7)
    rest = x - hi
    mid = lax.reduce_precision(rest, exponent_bits=8, mantissa_bits=7)
    lo = rest - mid
    return jnp.concatenate([hi, mid, lo], axis=-1).astype(jnp.bfloat16)


def join_three(x):
    n = x.shape[-1] // 3
    x = x.astype(jnp.float32)
    return (x[..., :n] + x[..., n : 2 * n]) + x[..., 2 * n :]


def on_device(
    query,
    new_key,
    new_value,
    key_pool,
    value_pool,
    long_key,
    long_value,
    serve_table,
    serve_len,
    page_slot,
    page_offset,
    long_request,
    long_len,
    lambda_head,
    norm_gain,
    out_weight,
):
    req_count = query.shape[0]
    serve_count = serve_table.shape[0]
    long_count = long_request.shape[0]
    seq_index = lax.axis_index("seq")
    seq_count = lax.axis_size("seq")
    tp_count = lax.axis_size("tp")
    all_queries = lax.all_to_all(
        jnp.broadcast_to(query[None], (seq_count,) + query.shape), "seq", 0, 0, tiled=True
    ).reshape(-1, 2, DH)
    slot_queries = all_queries[jnp.maximum(serve_table, 0)]
    safe_slot = jnp.maximum(page_slot, 0)
    cell_pos = page_offset[:, None] + jnp.arange(key_pool.shape[1])[None, :]
    live = (page_slot[:, None] >= 0) & (cell_pos < serve_len[safe_slot][:, None])
    pool_max, pool_sum, pool_num = page_terms(key_pool, value_pool, slot_queries[safe_slot], live)
    slot_max, slot_sum, slot_num = fold_pages(pool_max, pool_sum, pool_num, page_slot, serve_count)
    long_cells = long_key.shape[1]
    per_long = long_cells // PG
    long_pages = long_count * per_long
    long_queries = jnp.repeat(all_queries[long_request], per_long, axis=0)
    long_pos = seq_index * long_cells + jnp.arange(long_cells)
    long_live = (long_pos[None, :] < long_len[:, None]).reshape(long_pages, PG)
    part_max, part_sum, part_num = page_terms(
        long_key.reshape(long_pages, PG, -1),
        long_value.reshape(long_pages, PG, -1),
        long_queries,
        long_live,
    )
    long_owner = jnp.repeat(jnp.arange(long_count), per_long)
    long_max, long_sum, long_num = fold_pages(part_max, part_sum, part_num, long_owner, long_count)
    row_max = jnp.concatenate([slot_max, long_max], axis=0)
    row_sum = jnp.concatenate([slot_sum, long_sum], axis=0)
    row_num = jnp.concatenate([slot_num, long_num], axis=0)
    row_req = jnp.concatenate([serve_table, long_request], axis=0)
    row_count = row_req.shape[0]
    width = 2 * DV + 128
    stats = jnp.concatenate([row_max, row_sum], axis=1)
    pieces = split_three(stats)
    packed = jnp.concatenate(
        [
            row_num.reshape(row_count, 2 * DV).astype(jnp.bfloat16),
            pieces,
            jnp.zeros((row_count, width - 2 * DV - pieces.shape[1]), jnp.bfloat16),
        ],
        axis=1,
    )
    empty_stats = split_three(
        jnp.concatenate([jnp.full((1, 2), MASKED, jnp.float32), jnp.zeros((1, 2), jnp.float32)], axis=1)
    )
    empty = jnp.concatenate(
        [
            jnp.zeros((1, 2 * DV), jnp.bfloat16),
            empty_stats,
            jnp.zeros((1, width - 2 * DV - empty_stats.shape[1]), jnp.bfloat16),
        ],
        axis=1,
    )
    total = seq_count * req_count
    target = jnp.where(row_req >= 0, row_req, total)
    outbox = jnp.broadcast_to(empty, (total + 1, width)).at[target].set(packed)[:total]
    inbox = lax.all_to_all(
        outbox.reshape(seq_count, req_count, width), "seq", 0, 0, tiled=True
    )
    in_num = inbox[:, :, : 2 * DV].astype(jnp.float32).reshape(seq_count, req_count, 2, DV)
    in_stats = join_three(inbox[:, :, 2 * DV : 2 * DV + 12])
    in_max = in_stats[:, :, 0:2]
    in_sum = in_stats[:, :, 2:4]
    own_queries = query.reshape(req_count, 2, DH)
    own_keys = new_key.reshape(req_count, 2, DH)
    own_scores = jnp.einsum(
        "rjd,rjd->rj", own_queries, own_keys, preferred_element_type=jnp.float32
    ) * DH ** (-0.5)
    best = jnp.maximum(own_scores, jnp.max(in_max, axis=0))
    factor = jnp.exp(in_max - best[None])
    own_weight = jnp.exp(own_scores - best)
    denom = own_weight + jnp.sum(factor * in_sum, axis=0)
    numer = own_weight[..., None] * new_value.reshape(req_count, 1, DV).astype(jnp.float32)
    numer = numer + jnp.sum(factor[..., None] * in_num, axis=0)
    attn = numer / denom[..., None]
    diff = attn[:, 0] - lambda_head[0] * attn[:, 1]
    normed = (
        diff
        * lax.rsqrt(jnp.mean(diff * diff, axis=-1, keepdims=True) + 1e-05)
        * norm_gain.reshape(1, DV)
    )
    normed = normed.astype(jnp.bfloat16)
    partial_out = jnp.dot(normed, out_weight, preferred_element_type=jnp.float32)
    cols = partial_out.shape[1] // tp_count
    pieces = lax.all_to_all(
        partial_out.reshape(req_count, tp_count, cols).transpose(1, 0, 2), "tp", 0, 0, tiled=True
    )
    return jnp.sum(pieces, axis=0).astype(jnp.bfloat16)


def solution(mesh):
    return jax.shard_map(
        on_device,
        mesh=mesh,
        in_specs=(
            P("seq", "tp"),
            P("seq", "tp"),
            P("seq", "tp"),
            P("seq", None, "tp"),
            P("seq", None, "tp"),
            P(None, "seq", "tp"),
            P(None, "seq", "tp"),
            P("seq"),
            P("seq"),
            P("seq"),
            P("seq"),
            P(),
            P(),
            P("tp"),
            P("tp"),
            P("tp", None),
        ),
        out_specs=P("seq", "tp"),
        check_vma=False,
    )
```

```python
import jax
import jax.numpy as jnp
from jax import lax
import functools

from jax.experimental import pallas as pl
from jax.sharding import PartitionSpec as P

DH = 128
DV = 256
PG = 64


MASKED = -1e30


def _terms_kernel(ohq_ref, q_ref, kp_ref, vp_ref, lk_ref, lv_ref, livep_ref, livel_ref,
                  max_ref, sum_ref, num_ref, *, pool_pages, long_pages, cells):
    pages = pool_pages + long_pages
    rows = 2 * pages
    qg = jnp.dot(ohq_ref[...], q_ref[...], preferred_element_type=jnp.float32)
    row = lax.broadcasted_iota(jnp.int32, qg.shape, 0)
    lane = lax.broadcasted_iota(jnp.int32, qg.shape, 1)
    keep = (lane < DH) == (row < pages)
    qsel = jnp.where(keep, qg, 0.0).astype(jnp.bfloat16)
    dims = (((1,), (1,)), ((), ()))
    s_pool = lax.dot_general(qsel, kp_ref[...], dims, preferred_element_type=jnp.float32) * DH ** (-0.5)
    s_long = lax.dot_general(qsel, lk_ref[...], dims, preferred_element_type=jnp.float32) * DH ** (-0.5)
    rp = lax.broadcasted_iota(jnp.int32, s_pool.shape, 0) % pages
    cp = lax.broadcasted_iota(jnp.int32, s_pool.shape, 1) // cells
    mask_pool = (rp == cp) & (livep_ref[...] > 0.0)
    rl = lax.broadcasted_iota(jnp.int32, s_long.shape, 0) % pages
    cl = lax.broadcasted_iota(jnp.int32, s_long.shape, 1) // cells + pool_pages
    mask_long = (rl == cl) & (livel_ref[...] > 0.0)
    s_pool = jnp.where(mask_pool, s_pool, MASKED)
    s_long = jnp.where(mask_long, s_long, MASKED)
    m = jnp.maximum(jnp.max(s_pool, axis=1, keepdims=True), jnp.max(s_long, axis=1, keepdims=True))
    w_pool = jnp.where(mask_pool, jnp.exp(s_pool - m), 0.0)
    w_long = jnp.where(mask_long, jnp.exp(s_long - m), 0.0)
    total = jnp.sum(w_pool, axis=1, keepdims=True) + jnp.sum(w_long, axis=1, keepdims=True)
    num = jnp.dot(w_pool.astype(jnp.bfloat16), vp_ref[...], preferred_element_type=jnp.float32)
    num = num + jnp.dot(w_long.astype(jnp.bfloat16), lv_ref[...], preferred_element_type=jnp.float32)
    max_ref[...] = jnp.broadcast_to(m, max_ref.shape)
    sum_ref[...] = jnp.broadcast_to(total, sum_ref.shape)
    num_ref[...] = num

def page_terms_kernel(ohq, q_all, kp, vp, lk, lv, livep, livel, cells, interpret=False):
    pool_pages = kp.shape[0] // cells
    long_pages = lk.shape[0] // cells
    rows = 2 * (pool_pages + long_pages)
    dv = vp.shape[1]
    kern = functools.partial(_terms_kernel, pool_pages=pool_pages, long_pages=long_pages, cells=cells)
    return pl.pallas_call(
        kern,
        out_shape=(
            jax.ShapeDtypeStruct((rows, 128), jnp.float32),
            jax.ShapeDtypeStruct((rows, 128), jnp.float32),
            jax.ShapeDtypeStruct((rows, dv), jnp.float32),
        ),
        interpret=interpret,
    )(ohq, q_all, kp, vp, lk, lv, livep, livel)


def fold_pages(page_max, page_sum, page_num, owners, group_count):
    member = (owners[:, None] == jnp.arange(group_count)[None, :])[:, :, None]
    group_max = jnp.max(jnp.where(member, page_max[:, None], MASKED), axis=0)
    factor = jnp.where(
        member, jnp.exp(jnp.where(member, page_max[:, None] - group_max[None], 0.0)), 0.0
    )
    group_sum = jnp.einsum("pgj,pj->gj", factor, page_sum, precision=lax.Precision.HIGHEST)
    group_num = jnp.einsum("pgj,pjv->gjv", factor, page_num, precision=lax.Precision.HIGHEST)
    return (group_max, group_sum, group_num)


def split_three(x):
    hi = lax.reduce_precision(x, exponent_bits=8, mantissa_bits=7)
    rest = x - hi
    mid = lax.reduce_precision(rest, exponent_bits=8, mantissa_bits=7)
    lo = rest - mid
    return jnp.concatenate([hi, mid, lo], axis=-1).astype(jnp.bfloat16)


def join_three(x):
    n = x.shape[-1] // 3
    x = x.astype(jnp.float32)
    return (x[..., :n] + x[..., n : 2 * n]) + x[..., 2 * n :]


def on_device(
    query,
    new_key,
    new_value,
    key_pool,
    value_pool,
    long_key,
    long_value,
    serve_table,
    serve_len,
    page_slot,
    page_offset,
    long_request,
    long_len,
    lambda_head,
    norm_gain,
    out_weight,
):
    req_count = query.shape[0]
    serve_count = serve_table.shape[0]
    long_count = long_request.shape[0]
    seq_index = lax.axis_index("seq")
    seq_count = lax.axis_size("seq")
    tp_count = lax.axis_size("tp")
    all_queries = lax.all_to_all(
        jnp.broadcast_to(query[None], (seq_count,) + query.shape), "seq", 0, 0, tiled=True
    )
    all_queries = all_queries.reshape(-1, 2 * DH)
    total = seq_count * req_count
    pool_count = key_pool.shape[0]
    cell_count = key_pool.shape[1]
    long_cells = long_key.shape[1]
    per_long = long_cells // PG
    long_pages = long_count * per_long
    page_count = pool_count + long_pages
    safe_slot = jnp.maximum(page_slot, 0)
    cell_pos = page_offset[:, None] + jnp.arange(cell_count)[None, :]
    live = (page_slot[:, None] >= 0) & (cell_pos < serve_len[safe_slot][:, None])
    long_pos = seq_index * long_cells + jnp.arange(long_cells)
    long_live = long_pos[None, :] < long_len[:, None]
    page_req = jnp.concatenate(
        [jnp.maximum(serve_table[safe_slot], 0), jnp.repeat(long_request, per_long)], axis=0
    )
    pick = (jnp.tile(page_req, 2)[:, None] == jnp.arange(total)[None, :]).astype(jnp.bfloat16)
    page_max, page_sum, page_num = page_terms_kernel(
        pick,
        all_queries,
        key_pool.reshape(pool_count * cell_count, -1),
        value_pool.reshape(pool_count * cell_count, -1),
        long_key.reshape(long_count * long_cells, -1),
        long_value.reshape(long_count * long_cells, -1),
        live.reshape(1, -1).astype(jnp.float32),
        long_live.reshape(1, -1).astype(jnp.float32),
        cell_count,
    )
    page_max = page_max[:, 0].reshape(2, page_count).T
    page_sum = page_sum[:, 0].reshape(2, page_count).T
    page_num = page_num.reshape(2, page_count, DV).transpose(1, 0, 2)
    slot_max, slot_sum, slot_num = fold_pages(
        page_max[:pool_count], page_sum[:pool_count], page_num[:pool_count], page_slot, serve_count
    )
    long_owner = jnp.repeat(jnp.arange(long_count), per_long)
    long_max, long_sum, long_num = fold_pages(
        page_max[pool_count:], page_sum[pool_count:], page_num[pool_count:], long_owner, long_count
    )
    row_max = jnp.concatenate([slot_max, long_max], axis=0)
    row_sum = jnp.concatenate([slot_sum, long_sum], axis=0)
    row_num = jnp.concatenate([slot_num, long_num], axis=0)
    row_req = jnp.concatenate([serve_table, long_request], axis=0)
    row_count = row_req.shape[0]
    width = 2 * DV + 128
    stats = jnp.concatenate([row_max, row_sum], axis=1)
    pieces = split_three(stats)
    packed = jnp.concatenate(
        [
            row_num.reshape(row_count, 2 * DV).astype(jnp.bfloat16),
            pieces,
            jnp.zeros((row_count, width - 2 * DV - pieces.shape[1]), jnp.bfloat16),
        ],
        axis=1,
    )
    empty_stats = split_three(
        jnp.concatenate([jnp.full((1, 2), MASKED, jnp.float32), jnp.zeros((1, 2), jnp.float32)], axis=1)
    )
    empty = jnp.concatenate(
        [
            jnp.zeros((1, 2 * DV), jnp.bfloat16),
            empty_stats,
            jnp.zeros((1, width - 2 * DV - empty_stats.shape[1]), jnp.bfloat16),
        ],
        axis=1,
    )
    target = jnp.where(row_req >= 0, row_req, total)
    outbox = jnp.broadcast_to(empty, (total + 1, width)).at[target].set(packed)[:total]
    inbox = lax.all_to_all(
        outbox.reshape(seq_count, req_count, width), "seq", 0, 0, tiled=True
    )
    in_num = inbox[:, :, : 2 * DV].astype(jnp.float32).reshape(seq_count, req_count, 2, DV)
    in_stats = join_three(inbox[:, :, 2 * DV : 2 * DV + 12])
    in_max = in_stats[:, :, 0:2]
    in_sum = in_stats[:, :, 2:4]
    own_queries = query.reshape(req_count, 2, DH)
    own_keys = new_key.reshape(req_count, 2, DH)
    own_scores = jnp.einsum(
        "rjd,rjd->rj", own_queries, own_keys, preferred_element_type=jnp.float32
    ) * DH ** (-0.5)
    best = jnp.maximum(own_scores, jnp.max(in_max, axis=0))
    factor = jnp.exp(in_max - best[None])
    own_weight = jnp.exp(own_scores - best)
    denom = own_weight + jnp.sum(factor * in_sum, axis=0)
    numer = own_weight[..., None] * new_value.reshape(req_count, 1, DV).astype(jnp.float32)
    numer = numer + jnp.sum(factor[..., None] * in_num, axis=0)
    attn = numer / denom[..., None]
    diff = attn[:, 0] - lambda_head[0] * attn[:, 1]
    normed = (
        diff
        * lax.rsqrt(jnp.mean(diff * diff, axis=-1, keepdims=True) + 1e-05)
        * norm_gain.reshape(1, DV)
    )
    normed = normed.astype(jnp.bfloat16)
    partial_out = jnp.dot(normed, out_weight, preferred_element_type=jnp.float32)
    cols = partial_out.shape[1] // tp_count
    pieces = lax.all_to_all(
        partial_out.reshape(req_count, tp_count, cols).transpose(1, 0, 2), "tp", 0, 0, tiled=True
    )
    return jnp.sum(pieces, axis=0).astype(jnp.bfloat16)


def solution(mesh):
    return jax.shard_map(
        on_device,
        mesh=mesh,
        in_specs=(
            P("seq", "tp"),
            P("seq", "tp"),
            P("seq", "tp"),
            P("seq", None, "tp"),
            P("seq", None, "tp"),
            P(None, "seq", "tp"),
            P(None, "seq", "tp"),
            P("seq"),
            P("seq"),
            P("seq"),
            P("seq"),
            P(),
            P(),
            P("tp"),
            P("tp"),
            P("tp", None),
        ),
        out_specs=P("seq", "tp"),
        check_vma=False,
    )
```

```python
import jax
import jax.numpy as jnp
from jax import lax
import functools

from jax.experimental import pallas as pl
from jax.sharding import PartitionSpec as P

DH = 128
DV = 256
PG = 64


MASKED = -1e30


def _outbox_kernel(pick_ref, q_ref, kp_ref, vp_ref, lk_ref, lv_ref, colp_ref, coll_ref, place_ref,
                   out_ref, *, groups):
    qg = jnp.dot(pick_ref[...], q_ref[...], preferred_element_type=jnp.float32)
    row = lax.broadcasted_iota(jnp.int32, qg.shape, 0)
    lane = lax.broadcasted_iota(jnp.int32, qg.shape, 1)
    keep = (lane < DH) == (row < groups)
    qsel = jnp.where(keep, qg, 0.0).astype(jnp.bfloat16)
    dims = (((1,), (1,)), ((), ()))
    s_pool = lax.dot_general(qsel, kp_ref[...], dims, preferred_element_type=jnp.float32) * DH ** (-0.5)
    s_long = lax.dot_general(qsel, lk_ref[...], dims, preferred_element_type=jnp.float32) * DH ** (-0.5)
    own = lax.broadcasted_iota(jnp.int32, (2 * groups, 1), 0)
    own = jnp.where(own < groups, own, own - groups)
    mask_pool = own == colp_ref[...]
    mask_long = own == coll_ref[...]
    s_pool = jnp.where(mask_pool, s_pool, MASKED)
    s_long = jnp.where(mask_long, s_long, MASKED)
    m = jnp.maximum(jnp.max(s_pool, axis=1, keepdims=True), jnp.max(s_long, axis=1, keepdims=True))
    w_pool = jnp.where(mask_pool, jnp.exp(s_pool - m), 0.0)
    w_long = jnp.where(mask_long, jnp.exp(s_long - m), 0.0)
    total = jnp.sum(w_pool, axis=1, keepdims=True) + jnp.sum(w_long, axis=1, keepdims=True)
    num = jnp.dot(w_pool.astype(jnp.bfloat16), vp_ref[...], preferred_element_type=jnp.float32)
    num = num + jnp.dot(w_long.astype(jnp.bfloat16), lv_ref[...], preferred_element_type=jnp.float32)
    numb = num.astype(jnp.bfloat16)
    stats = (m[:groups], m[groups:], total[:groups], total[groups:])
    slane = lax.broadcasted_iota(jnp.int32, (groups, 128), 1)
    block = jnp.zeros((groups, 128), jnp.float32)
    for k, x in enumerate(stats):
        hi = x.astype(jnp.bfloat16).astype(jnp.float32)
        rest = x - hi
        mid = rest.astype(jnp.bfloat16).astype(jnp.float32)
        lo = rest - mid
        for piece, value in enumerate((hi, mid, lo)):
            block = jnp.where(slane == piece * 4 + k, value, block)
    packed = jnp.concatenate(
        [numb[:groups], numb[groups:], block.astype(jnp.bfloat16)], axis=1
    )
    out_ref[...] = jnp.dot(place_ref[...], packed, preferred_element_type=jnp.float32).astype(out_ref.dtype)


def outbox_kernel(pick, q_all, kp, vp, lk, lv, colp, coll, place, width, interpret=False):
    groups = place.shape[1]
    kern = functools.partial(_outbox_kernel, groups=groups)
    return pl.pallas_call(
        kern,
        out_shape=jax.ShapeDtypeStruct((place.shape[0], width), jnp.bfloat16),
        interpret=interpret,
    )(pick, q_all, kp, vp, lk, lv, colp, coll, place)


def join_three(x):
    n = x.shape[-1] // 3
    x = x.astype(jnp.float32)
    return (x[..., :n] + x[..., n : 2 * n]) + x[..., 2 * n :]


def on_device(
    query,
    new_key,
    new_value,
    key_pool,
    value_pool,
    long_key,
    long_value,
    serve_table,
    serve_len,
    page_slot,
    page_offset,
    long_request,
    long_len,
    lambda_head,
    norm_gain,
    out_weight,
):
    req_count = query.shape[0]
    serve_count = serve_table.shape[0]
    long_count = long_request.shape[0]
    seq_index = lax.axis_index("seq")
    seq_count = lax.axis_size("seq")
    tp_count = lax.axis_size("tp")
    all_queries = lax.all_to_all(
        jnp.broadcast_to(query[None], (seq_count,) + query.shape), "seq", 0, 0, tiled=True
    )
    all_queries = all_queries.reshape(-1, 2 * DH)
    total = seq_count * req_count
    pool_count = key_pool.shape[0]
    cell_count = key_pool.shape[1]
    long_cells = long_key.shape[1]
    groups = 16
    width = 2 * DV + 128
    safe_slot = jnp.maximum(page_slot, 0)
    cell_pos = page_offset[:, None] + jnp.arange(cell_count)[None, :]
    live = (page_slot[:, None] >= 0) & (cell_pos < serve_len[safe_slot][:, None])
    pool_group = jnp.where(live, page_slot[:, None], -1).reshape(1, -1)
    long_pos = seq_index * long_cells + jnp.arange(long_cells)
    long_live = long_pos[None, :] < long_len[:, None]
    long_group = jnp.where(long_live, serve_count + jnp.arange(long_count)[:, None], -1).reshape(1, -1)
    row_req = jnp.concatenate([serve_table, long_request], axis=0)
    row_req = jnp.concatenate([row_req, jnp.full((groups - row_req.shape[0],), -1, row_req.dtype)])
    pick = (jnp.tile(jnp.maximum(row_req, 0), 2)[:, None] == jnp.arange(total)[None, :])
    hit = row_req[None, :] == jnp.arange(total)[:, None]
    place = hit.at[:, groups - 1].set(jnp.logical_not(jnp.any(hit, axis=1)))
    outbox = outbox_kernel(
        pick.astype(jnp.bfloat16),
        all_queries,
        key_pool.reshape(pool_count * cell_count, -1),
        value_pool.reshape(pool_count * cell_count, -1),
        long_key.reshape(long_count * long_cells, -1),
        long_value.reshape(long_count * long_cells, -1),
        pool_group.astype(jnp.int32),
        long_group.astype(jnp.int32),
        place.astype(jnp.bfloat16),
        width,
    )
    inbox = lax.all_to_all(
        outbox.reshape(seq_count, req_count, width), "seq", 0, 0, tiled=True
    )
    in_num = inbox[:, :, : 2 * DV].astype(jnp.float32).reshape(seq_count, req_count, 2, DV)
    in_stats = join_three(inbox[:, :, 2 * DV : 2 * DV + 12])
    in_max = in_stats[:, :, 0:2]
    in_sum = in_stats[:, :, 2:4]
    own_queries = query.reshape(req_count, 2, DH)
    own_keys = new_key.reshape(req_count, 2, DH)
    own_scores = jnp.einsum(
        "rjd,rjd->rj", own_queries, own_keys, preferred_element_type=jnp.float32
    ) * DH ** (-0.5)
    best = jnp.maximum(own_scores, jnp.max(in_max, axis=0))
    factor = jnp.exp(in_max - best[None])
    own_weight = jnp.exp(own_scores - best)
    denom = own_weight + jnp.sum(factor * in_sum, axis=0)
    numer = own_weight[..., None] * new_value.reshape(req_count, 1, DV).astype(jnp.float32)
    numer = numer + jnp.sum(factor[..., None] * in_num, axis=0)
    attn = numer / denom[..., None]
    diff = attn[:, 0] - lambda_head[0] * attn[:, 1]
    normed = (
        diff
        * lax.rsqrt(jnp.mean(diff * diff, axis=-1, keepdims=True) + 1e-05)
        * norm_gain.reshape(1, DV)
    )
    normed = normed.astype(jnp.bfloat16)
    partial_out = jnp.dot(normed, out_weight, preferred_element_type=jnp.float32)
    cols = partial_out.shape[1] // tp_count
    pieces = lax.all_to_all(
        partial_out.reshape(req_count, tp_count, cols).transpose(1, 0, 2), "tp", 0, 0, tiled=True
    )
    return jnp.sum(pieces, axis=0).astype(jnp.bfloat16)


def solution(mesh):
    return jax.shard_map(
        on_device,
        mesh=mesh,
        in_specs=(
            P("seq", "tp"),
            P("seq", "tp"),
            P("seq", "tp"),
            P("seq", None, "tp"),
            P("seq", None, "tp"),
            P(None, "seq", "tp"),
            P(None, "seq", "tp"),
            P("seq"),
            P("seq"),
            P("seq"),
            P("seq"),
            P(),
            P(),
            P("tp"),
            P("tp"),
            P("tp", None),
        ),
        out_specs=P("seq", "tp"),
        check_vma=False,
    )
```

```python
import jax
import jax.numpy as jnp
from jax import lax
import functools

from jax.experimental import pallas as pl
from jax.experimental.pallas import tpu as pltpu
from jax.sharding import PartitionSpec as P

DH = 128
DV = 256
PG = 64


MASKED = -1e30


def _outbox_kernel(pick_ref, q_ref, kp_hbm, vp_hbm, lk_hbm, lv_hbm, colp_ref, coll_ref, place_ref,
                   out_ref, kp_ref, vp_ref, lk_ref, lv_ref, sems, *, groups):
    loads = [
        pltpu.make_async_copy(src, dst, sems.at[i])
        for i, (src, dst) in enumerate(
            ((kp_hbm, kp_ref), (lk_hbm, lk_ref), (vp_hbm, vp_ref), (lv_hbm, lv_ref))
        )
    ]
    for load in loads:
        load.start()
    qg = jnp.dot(pick_ref[...], q_ref[...], preferred_element_type=jnp.float32)
    row = lax.broadcasted_iota(jnp.int32, qg.shape, 0)
    lane = lax.broadcasted_iota(jnp.int32, qg.shape, 1)
    keep = (lane < DH) == (row < groups)
    qsel = jnp.where(keep, qg, 0.0).astype(jnp.bfloat16)
    dims = (((1,), (1,)), ((), ()))
    loads[0].wait()
    s_pool = lax.dot_general(qsel, kp_ref[...], dims, preferred_element_type=jnp.float32) * DH ** (-0.5)
    loads[1].wait()
    s_long = lax.dot_general(qsel, lk_ref[...], dims, preferred_element_type=jnp.float32) * DH ** (-0.5)
    own = lax.broadcasted_iota(jnp.int32, (2 * groups, 1), 0)
    own = jnp.where(own < groups, own, own - groups)
    mask_pool = own == colp_ref[...]
    mask_long = own == coll_ref[...]
    s_pool = jnp.where(mask_pool, s_pool, MASKED)
    s_long = jnp.where(mask_long, s_long, MASKED)
    m = jnp.maximum(jnp.max(s_pool, axis=1, keepdims=True), jnp.max(s_long, axis=1, keepdims=True))
    w_pool = jnp.where(mask_pool, jnp.exp(s_pool - m), 0.0)
    w_long = jnp.where(mask_long, jnp.exp(s_long - m), 0.0)
    total = jnp.sum(w_pool, axis=1, keepdims=True) + jnp.sum(w_long, axis=1, keepdims=True)
    loads[2].wait()
    num = jnp.dot(w_pool.astype(jnp.bfloat16), vp_ref[...], preferred_element_type=jnp.float32)
    loads[3].wait()
    num = num + jnp.dot(w_long.astype(jnp.bfloat16), lv_ref[...], preferred_element_type=jnp.float32)
    numb = num.astype(jnp.bfloat16)
    stats = (m[:groups], m[groups:], total[:groups], total[groups:])
    slane = lax.broadcasted_iota(jnp.int32, (groups, 128), 1)
    block = jnp.zeros((groups, 128), jnp.float32)
    for k, x in enumerate(stats):
        hi = x.astype(jnp.bfloat16).astype(jnp.float32)
        rest = x - hi
        mid = rest.astype(jnp.bfloat16).astype(jnp.float32)
        lo = rest - mid
        for piece, value in enumerate((hi, mid, lo)):
            block = jnp.where(slane == piece * 4 + k, value, block)
    packed = jnp.concatenate(
        [numb[:groups], numb[groups:], block.astype(jnp.bfloat16)], axis=1
    )
    out_ref[...] = jnp.dot(place_ref[...], packed, preferred_element_type=jnp.float32).astype(out_ref.dtype)


def outbox_kernel(pick, q_all, kp, vp, lk, lv, colp, coll, place, width, interpret=False):
    groups = place.shape[1]
    kern = functools.partial(_outbox_kernel, groups=groups)
    vmem = pl.BlockSpec(memory_space=pltpu.VMEM)
    hbm = pl.BlockSpec(memory_space=pl.ANY)
    return pl.pallas_call(
        kern,
        out_shape=jax.ShapeDtypeStruct((place.shape[0], width), jnp.bfloat16),
        in_specs=[vmem, vmem, hbm, hbm, hbm, hbm, vmem, vmem, vmem],
        out_specs=vmem,
        scratch_shapes=[
            pltpu.VMEM(kp.shape, kp.dtype),
            pltpu.VMEM(vp.shape, vp.dtype),
            pltpu.VMEM(lk.shape, lk.dtype),
            pltpu.VMEM(lv.shape, lv.dtype),
            pltpu.SemaphoreType.DMA((4,)),
        ],
        interpret=interpret,
    )(pick, q_all, kp, vp, lk, lv, colp, coll, place)


def join_three(x):
    n = x.shape[-1] // 3
    x = x.astype(jnp.float32)
    return (x[..., :n] + x[..., n : 2 * n]) + x[..., 2 * n :]


def on_device(
    query,
    new_key,
    new_value,
    key_pool,
    value_pool,
    long_key,
    long_value,
    serve_table,
    serve_len,
    page_slot,
    page_offset,
    long_request,
    long_len,
    lambda_head,
    norm_gain,
    out_weight,
):
    req_count = query.shape[0]
    serve_count = serve_table.shape[0]
    long_count = long_request.shape[0]
    seq_index = lax.axis_index("seq")
    seq_count = lax.axis_size("seq")
    tp_count = lax.axis_size("tp")
    all_queries = lax.all_to_all(
        jnp.broadcast_to(query[None], (seq_count,) + query.shape), "seq", 0, 0, tiled=True
    )
    all_queries = all_queries.reshape(-1, 2 * DH)
    total = seq_count * req_count
    pool_count = key_pool.shape[0]
    cell_count = key_pool.shape[1]
    long_cells = long_key.shape[1]
    groups = 16
    width = 2 * DV + 128
    safe_slot = jnp.maximum(page_slot, 0)
    cell_pos = page_offset[:, None] + jnp.arange(cell_count)[None, :]
    live = (page_slot[:, None] >= 0) & (cell_pos < serve_len[safe_slot][:, None])
    pool_group = jnp.where(live, page_slot[:, None], -1).reshape(1, -1)
    long_pos = seq_index * long_cells + jnp.arange(long_cells)
    long_live = long_pos[None, :] < long_len[:, None]
    long_group = jnp.where(long_live, serve_count + jnp.arange(long_count)[:, None], -1).reshape(1, -1)
    row_req = jnp.concatenate([serve_table, long_request], axis=0)
    row_req = jnp.concatenate([row_req, jnp.full((groups - row_req.shape[0],), -1, row_req.dtype)])
    pick = (jnp.tile(jnp.maximum(row_req, 0), 2)[:, None] == jnp.arange(total)[None, :])
    hit = row_req[None, :] == jnp.arange(total)[:, None]
    place = hit.at[:, groups - 1].set(jnp.logical_not(jnp.any(hit, axis=1)))
    outbox = outbox_kernel(
        pick.astype(jnp.bfloat16),
        all_queries,
        key_pool.reshape(pool_count * cell_count, -1),
        value_pool.reshape(pool_count * cell_count, -1),
        long_key.reshape(long_count * long_cells, -1),
        long_value.reshape(long_count * long_cells, -1),
        pool_group.astype(jnp.int32),
        long_group.astype(jnp.int32),
        place.astype(jnp.bfloat16),
        width,
    )
    inbox = lax.all_to_all(
        outbox.reshape(seq_count, req_count, width), "seq", 0, 0, tiled=True
    )
    in_num = inbox[:, :, : 2 * DV].astype(jnp.float32).reshape(seq_count, req_count, 2, DV)
    in_stats = join_three(inbox[:, :, 2 * DV : 2 * DV + 12])
    in_max = in_stats[:, :, 0:2]
    in_sum = in_stats[:, :, 2:4]
    own_queries = query.reshape(req_count, 2, DH)
    own_keys = new_key.reshape(req_count, 2, DH)
    own_scores = jnp.einsum(
        "rjd,rjd->rj", own_queries, own_keys, preferred_element_type=jnp.float32
    ) * DH ** (-0.5)
    best = jnp.maximum(own_scores, jnp.max(in_max, axis=0))
    factor = jnp.exp(in_max - best[None])
    own_weight = jnp.exp(own_scores - best)
    denom = own_weight + jnp.sum(factor * in_sum, axis=0)
    numer = own_weight[..., None] * new_value.reshape(req_count, 1, DV).astype(jnp.float32)
    numer = numer + jnp.sum(factor[..., None] * in_num, axis=0)
    attn = numer / denom[..., None]
    diff = attn[:, 0] - lambda_head[0] * attn[:, 1]
    normed = (
        diff
        * lax.rsqrt(jnp.mean(diff * diff, axis=-1, keepdims=True) + 1e-05)
        * norm_gain.reshape(1, DV)
    )
    normed = normed.astype(jnp.bfloat16)
    partial_out = jnp.dot(normed, out_weight, preferred_element_type=jnp.float32)
    cols = partial_out.shape[1] // tp_count
    pieces = lax.all_to_all(
        partial_out.reshape(req_count, tp_count, cols).transpose(1, 0, 2), "tp", 0, 0, tiled=True
    )
    return jnp.sum(pieces, axis=0).astype(jnp.bfloat16)


def solution(mesh):
    return jax.shard_map(
        on_device,
        mesh=mesh,
        in_specs=(
            P("seq", "tp"),
            P("seq", "tp"),
            P("seq", "tp"),
            P("seq", None, "tp"),
            P("seq", None, "tp"),
            P(None, "seq", "tp"),
            P(None, "seq", "tp"),
            P("seq"),
            P("seq"),
            P("seq"),
            P("seq"),
            P(),
            P(),
            P("tp"),
            P("tp"),
            P("tp", None),
        ),
        out_specs=P("seq", "tp"),
        check_vma=False,
    )
```

```python
import jax
import jax.numpy as jnp
from jax import lax
import functools

from jax.experimental import pallas as pl
from jax.experimental.pallas import tpu as pltpu
from jax.sharding import PartitionSpec as P

DH = 128
DV = 256
PG = 64


MASKED = -1e30


def _outbox_kernel(pick_ref, q_ref, kp_ref, vp_ref, lk_ref, lv_ref, colp_ref, coll_ref, place_ref,
                   out_ref, *, groups):
    qg = jnp.dot(pick_ref[...], q_ref[...], preferred_element_type=jnp.float32)
    row = lax.broadcasted_iota(jnp.int32, qg.shape, 0)
    lane = lax.broadcasted_iota(jnp.int32, qg.shape, 1)
    keep = (lane < DH) == (row < groups)
    qsel = jnp.where(keep, qg, 0.0).astype(jnp.bfloat16)
    dims = (((1,), (1,)), ((), ()))
    s_pool = lax.dot_general(qsel, kp_ref[...], dims, preferred_element_type=jnp.float32) * DH ** (-0.5)
    s_long = lax.dot_general(qsel, lk_ref[...], dims, preferred_element_type=jnp.float32) * DH ** (-0.5)
    own = lax.broadcasted_iota(jnp.int32, (2 * groups, 1), 0)
    own = jnp.where(own < groups, own, own - groups)
    mask_pool = own == colp_ref[...]
    mask_long = own == coll_ref[...]
    s_pool = jnp.where(mask_pool, s_pool, MASKED)
    s_long = jnp.where(mask_long, s_long, MASKED)
    m = jnp.maximum(jnp.max(s_pool, axis=1, keepdims=True), jnp.max(s_long, axis=1, keepdims=True))
    w_pool = jnp.where(mask_pool, jnp.exp(s_pool - m), 0.0)
    w_long = jnp.where(mask_long, jnp.exp(s_long - m), 0.0)
    total = jnp.sum(w_pool, axis=1, keepdims=True) + jnp.sum(w_long, axis=1, keepdims=True)
    num = jnp.dot(w_pool.astype(jnp.bfloat16), vp_ref[...], preferred_element_type=jnp.float32)
    num = num + jnp.dot(w_long.astype(jnp.bfloat16), lv_ref[...], preferred_element_type=jnp.float32)
    numb = num.astype(jnp.bfloat16)
    stats = (m[:groups], m[groups:], total[:groups], total[groups:])
    slane = lax.broadcasted_iota(jnp.int32, (groups, 128), 1)
    block = jnp.zeros((groups, 128), jnp.float32)
    for k, x in enumerate(stats):
        hi = x.astype(jnp.bfloat16).astype(jnp.float32)
        rest = x - hi
        mid = rest.astype(jnp.bfloat16).astype(jnp.float32)
        lo = rest - mid
        for piece, value in enumerate((hi, mid, lo)):
            block = jnp.where(slane == piece * 4 + k, value, block)
    packed = jnp.concatenate(
        [numb[:groups], numb[groups:], block.astype(jnp.bfloat16)], axis=1
    )
    out_ref[...] = jnp.dot(place_ref[...], packed, preferred_element_type=jnp.float32).astype(out_ref.dtype)


def outbox_kernel(pick, q_all, kp, vp, lk, lv, colp, coll, place, width, interpret=False):
    groups = place.shape[1]
    kern = functools.partial(_outbox_kernel, groups=groups)
    return pl.pallas_call(
        kern,
        out_shape=jax.ShapeDtypeStruct((place.shape[0], width), jnp.bfloat16),
        interpret=interpret,
    )(pick, q_all, kp, vp, lk, lv, colp, coll, place)


def _combine_kernel(inbox_ref, q_ref, k_ref, v_ref, lam_ref, gain_ref, w_ref, out_ref):
    x = inbox_ref[...]
    sources, reqs, _ = x.shape
    dv = v_ref.shape[1]
    half = q_ref.shape[1] // 2
    stats = x[:, :, 2 * dv :].astype(jnp.float32)
    width = stats.shape[2]
    dec = (stats + pltpu.roll(stats, width - 4, 2)) + pltpu.roll(stats, width - 8, 2)
    in_sum = pltpu.roll(dec, width - 2, 2)
    prod = q_ref[...].astype(jnp.float32) * k_ref[...].astype(jnp.float32)
    s0 = jnp.sum(prod[:, :half], axis=1, keepdims=True) * DH ** (-0.5)
    s1 = jnp.sum(prod[:, half:], axis=1, keepdims=True) * DH ** (-0.5)
    lane = lax.broadcasted_iota(jnp.int32, (reqs, width), 1)
    own = jnp.where(lane == 0, s0, jnp.where(lane == 1, s1, 0.0))
    best = jnp.maximum(own, jnp.max(dec, axis=0))
    factor = jnp.exp(dec - best[None])
    own_w = jnp.exp(own - best)
    denom = own_w + jnp.sum(factor * in_sum, axis=0)
    value = v_ref[...].astype(jnp.float32)
    attn = []
    for j in range(2):
        f = jnp.broadcast_to(factor[:, :, j : j + 1], (sources, reqs, dv))
        part = x[:, :, j * dv : (j + 1) * dv].astype(jnp.float32)
        numer = own_w[:, j : j + 1] * value + jnp.sum(f * part, axis=0)
        attn.append(numer / denom[:, j : j + 1])
    diff = attn[0] - lam_ref[0, 0] * attn[1]
    normed = diff * lax.rsqrt(jnp.mean(diff * diff, axis=-1, keepdims=True) + 1e-05) * gain_ref[...]
    res = jnp.dot(normed.astype(jnp.bfloat16), w_ref[...], preferred_element_type=jnp.float32)
    cols = out_ref.shape[2]
    for t in range(out_ref.shape[0]):
        out_ref[t] = res[:, t * cols : (t + 1) * cols]


def combine_kernel(inbox, q, k, v, lam, gain, w, parts, interpret=False):
    reqs = q.shape[0]
    cols = w.shape[1] // parts
    smem = pl.BlockSpec(memory_space=pltpu.SMEM)
    vmem = pl.BlockSpec(memory_space=pltpu.VMEM)
    return pl.pallas_call(
        _combine_kernel,
        out_shape=jax.ShapeDtypeStruct((parts, reqs, cols), jnp.float32),
        in_specs=[vmem, vmem, vmem, vmem, smem, vmem, vmem],
        out_specs=vmem,
        interpret=interpret,
    )(inbox, q, k, v, lam, gain, w)


def on_device(
    query,
    new_key,
    new_value,
    key_pool,
    value_pool,
    long_key,
    long_value,
    serve_table,
    serve_len,
    page_slot,
    page_offset,
    long_request,
    long_len,
    lambda_head,
    norm_gain,
    out_weight,
):
    req_count = query.shape[0]
    serve_count = serve_table.shape[0]
    long_count = long_request.shape[0]
    seq_index = lax.axis_index("seq")
    seq_count = lax.axis_size("seq")
    tp_count = lax.axis_size("tp")
    all_queries = lax.all_to_all(
        jnp.broadcast_to(query[None], (seq_count,) + query.shape), "seq", 0, 0, tiled=True
    )
    all_queries = all_queries.reshape(-1, 2 * DH)
    total = seq_count * req_count
    pool_count = key_pool.shape[0]
    cell_count = key_pool.shape[1]
    long_cells = long_key.shape[1]
    groups = 16
    width = 2 * DV + 128
    safe_slot = jnp.maximum(page_slot, 0)
    cell_pos = page_offset[:, None] + jnp.arange(cell_count)[None, :]
    live = (page_slot[:, None] >= 0) & (cell_pos < serve_len[safe_slot][:, None])
    pool_group = jnp.where(live, page_slot[:, None], -1).reshape(1, -1)
    long_pos = seq_index * long_cells + jnp.arange(long_cells)
    long_live = long_pos[None, :] < long_len[:, None]
    long_group = jnp.where(long_live, serve_count + jnp.arange(long_count)[:, None], -1).reshape(1, -1)
    row_req = jnp.concatenate([serve_table, long_request], axis=0)
    row_req = jnp.concatenate([row_req, jnp.full((groups - row_req.shape[0],), -1, row_req.dtype)])
    pick = (jnp.tile(jnp.maximum(row_req, 0), 2)[:, None] == jnp.arange(total)[None, :])
    hit = row_req[None, :] == jnp.arange(total)[:, None]
    place = hit.at[:, groups - 1].set(jnp.logical_not(jnp.any(hit, axis=1)))
    outbox = outbox_kernel(
        pick.astype(jnp.bfloat16),
        all_queries,
        key_pool.reshape(pool_count * cell_count, -1),
        value_pool.reshape(pool_count * cell_count, -1),
        long_key.reshape(long_count * long_cells, -1),
        long_value.reshape(long_count * long_cells, -1),
        pool_group.astype(jnp.int32),
        long_group.astype(jnp.int32),
        place.astype(jnp.bfloat16),
        width,
    )
    inbox = lax.all_to_all(
        outbox.reshape(seq_count, req_count, width), "seq", 0, 0, tiled=True
    )
    pieces = combine_kernel(
        inbox,
        query,
        new_key,
        new_value,
        lambda_head.reshape(1, 1),
        norm_gain.reshape(1, DV),
        out_weight,
        tp_count,
    )
    pieces = lax.all_to_all(pieces, "tp", 0, 0, tiled=True)
    return jnp.sum(pieces, axis=0).astype(jnp.bfloat16)


def solution(mesh):
    return jax.shard_map(
        on_device,
        mesh=mesh,
        in_specs=(
            P("seq", "tp"),
            P("seq", "tp"),
            P("seq", "tp"),
            P("seq", None, "tp"),
            P("seq", None, "tp"),
            P(None, "seq", "tp"),
            P(None, "seq", "tp"),
            P("seq"),
            P("seq"),
            P("seq"),
            P("seq"),
            P(),
            P(),
            P("tp"),
            P("tp"),
            P("tp", None),
        ),
        out_specs=P("seq", "tp"),
        check_vma=False,
    )
```

```python
import jax
import jax.numpy as jnp
from jax import lax
import functools

from jax.experimental import pallas as pl
from jax.experimental.pallas import tpu as pltpu
from jax.sharding import PartitionSpec as P

DH = 128
DV = 256
PG = 64


MASKED = -1e30


def _outbox_kernel(pick_ref, q_ref, kp_ref, vp_ref, lk_ref, lv_ref, colp_ref, coll_ref, place_ref,
                   out_ref, *, groups):
    qg = jnp.dot(pick_ref[...], q_ref[...], preferred_element_type=jnp.float32)
    row = lax.broadcasted_iota(jnp.int32, qg.shape, 0)
    lane = lax.broadcasted_iota(jnp.int32, qg.shape, 1)
    keep = (lane < DH) == (row < groups)
    qsel = jnp.where(keep, qg, 0.0).astype(jnp.bfloat16)
    dims = (((1,), (1,)), ((), ()))
    s_pool = lax.dot_general(qsel, kp_ref[...], dims, preferred_element_type=jnp.float32) * DH ** (-0.5)
    s_long = lax.dot_general(qsel, lk_ref[...], dims, preferred_element_type=jnp.float32) * DH ** (-0.5)
    own = lax.broadcasted_iota(jnp.int32, (2 * groups, 1), 0)
    own = jnp.where(own < groups, own, own - groups)
    mask_pool = own == colp_ref[...]
    mask_long = own == coll_ref[...]
    s_pool = jnp.where(mask_pool, s_pool, MASKED)
    s_long = jnp.where(mask_long, s_long, MASKED)
    m = jnp.maximum(jnp.max(s_pool, axis=1, keepdims=True), jnp.max(s_long, axis=1, keepdims=True))
    w_pool = jnp.where(mask_pool, jnp.exp(s_pool - m), 0.0)
    w_long = jnp.where(mask_long, jnp.exp(s_long - m), 0.0)
    total = jnp.sum(w_pool, axis=1, keepdims=True) + jnp.sum(w_long, axis=1, keepdims=True)
    num = jnp.dot(w_pool.astype(jnp.bfloat16), vp_ref[...], preferred_element_type=jnp.float32)
    num = num + jnp.dot(w_long.astype(jnp.bfloat16), lv_ref[...], preferred_element_type=jnp.float32)
    numb = num.astype(jnp.bfloat16)
    stats = (m[:groups], m[groups:], total[:groups], total[groups:])
    slane = lax.broadcasted_iota(jnp.int32, (groups, 128), 1)
    block = jnp.zeros((groups, 128), jnp.float32)
    for k, x in enumerate(stats):
        hi = x.astype(jnp.bfloat16).astype(jnp.float32)
        rest = x - hi
        mid = rest.astype(jnp.bfloat16).astype(jnp.float32)
        lo = rest - mid
        for piece, value in enumerate((hi, mid, lo)):
            block = jnp.where(slane == piece * 4 + k, value, block)
    packed = jnp.concatenate(
        [numb[:groups], numb[groups:], block.astype(jnp.bfloat16)], axis=1
    )
    out_ref[...] = jnp.dot(place_ref[...], packed, preferred_element_type=jnp.float32).astype(out_ref.dtype)


def outbox_kernel(pick, q_all, kp, vp, lk, lv, colp, coll, place, width, interpret=False):
    groups = place.shape[1]
    kern = functools.partial(_outbox_kernel, groups=groups)
    return pl.pallas_call(
        kern,
        out_shape=jax.ShapeDtypeStruct((place.shape[0], width), jnp.bfloat16),
        interpret=interpret,
    )(pick, q_all, kp, vp, lk, lv, colp, coll, place)


def _copies_kernel(x_ref, out_ref):
    out_ref[...] = jnp.broadcast_to(x_ref[...][None], out_ref.shape)


def copies_kernel(x, count):
    vmem = pl.BlockSpec(memory_space=pltpu.VMEM)
    return pl.pallas_call(
        _copies_kernel,
        out_shape=jax.ShapeDtypeStruct((count,) + x.shape, x.dtype),
        in_specs=[vmem],
        out_specs=vmem,
    )(x)


def join_three(x):
    n = x.shape[-1] // 3
    x = x.astype(jnp.float32)
    return (x[..., :n] + x[..., n : 2 * n]) + x[..., 2 * n :]


def on_device(
    query,
    new_key,
    new_value,
    key_pool,
    value_pool,
    long_key,
    long_value,
    serve_table,
    serve_len,
    page_slot,
    page_offset,
    long_request,
    long_len,
    lambda_head,
    norm_gain,
    out_weight,
):
    req_count = query.shape[0]
    serve_count = serve_table.shape[0]
    long_count = long_request.shape[0]
    seq_index = lax.axis_index("seq")
    seq_count = lax.axis_size("seq")
    tp_count = lax.axis_size("tp")
    all_queries = lax.all_to_all(
        copies_kernel(query, seq_count), "seq", 0, 0, tiled=True
    )
    all_queries = all_queries.reshape(-1, 2 * DH)
    total = seq_count * req_count
    pool_count = key_pool.shape[0]
    cell_count = key_pool.shape[1]
    long_cells = long_key.shape[1]
    groups = 16
    width = 2 * DV + 128
    safe_slot = jnp.maximum(page_slot, 0)
    cell_pos = page_offset[:, None] + jnp.arange(cell_count)[None, :]
    live = (page_slot[:, None] >= 0) & (cell_pos < serve_len[safe_slot][:, None])
    pool_group = jnp.where(live, page_slot[:, None], -1).reshape(1, -1)
    long_pos = seq_index * long_cells + jnp.arange(long_cells)
    long_live = long_pos[None, :] < long_len[:, None]
    long_group = jnp.where(long_live, serve_count + jnp.arange(long_count)[:, None], -1).reshape(1, -1)
    row_req = jnp.concatenate([serve_table, long_request], axis=0)
    row_req = jnp.concatenate([row_req, jnp.full((groups - row_req.shape[0],), -1, row_req.dtype)])
    pick = (jnp.tile(jnp.maximum(row_req, 0), 2)[:, None] == jnp.arange(total)[None, :])
    hit = row_req[None, :] == jnp.arange(total)[:, None]
    place = hit.at[:, groups - 1].set(jnp.logical_not(jnp.any(hit, axis=1)))
    outbox = outbox_kernel(
        pick.astype(jnp.bfloat16),
        all_queries,
        key_pool.reshape(pool_count * cell_count, -1),
        value_pool.reshape(pool_count * cell_count, -1),
        long_key.reshape(long_count * long_cells, -1),
        long_value.reshape(long_count * long_cells, -1),
        pool_group.astype(jnp.int32),
        long_group.astype(jnp.int32),
        place.astype(jnp.bfloat16),
        width,
    )
    inbox = lax.all_to_all(
        outbox.reshape(seq_count, req_count, width), "seq", 0, 0, tiled=True
    )
    in_num = inbox[:, :, : 2 * DV].astype(jnp.float32).reshape(seq_count, req_count, 2, DV)
    in_stats = join_three(inbox[:, :, 2 * DV : 2 * DV + 12])
    in_max = in_stats[:, :, 0:2]
    in_sum = in_stats[:, :, 2:4]
    own_queries = query.reshape(req_count, 2, DH)
    own_keys = new_key.reshape(req_count, 2, DH)
    own_scores = jnp.einsum(
        "rjd,rjd->rj", own_queries, own_keys, preferred_element_type=jnp.float32
    ) * DH ** (-0.5)
    best = jnp.maximum(own_scores, jnp.max(in_max, axis=0))
    factor = jnp.exp(in_max - best[None])
    own_weight = jnp.exp(own_scores - best)
    denom = own_weight + jnp.sum(factor * in_sum, axis=0)
    numer = own_weight[..., None] * new_value.reshape(req_count, 1, DV).astype(jnp.float32)
    numer = numer + jnp.sum(factor[..., None] * in_num, axis=0)
    attn = numer / denom[..., None]
    diff = attn[:, 0] - lambda_head[0] * attn[:, 1]
    normed = (
        diff
        * lax.rsqrt(jnp.mean(diff * diff, axis=-1, keepdims=True) + 1e-05)
        * norm_gain.reshape(1, DV)
    )
    normed = normed.astype(jnp.bfloat16)
    partial_out = jnp.dot(normed, out_weight, preferred_element_type=jnp.float32)
    cols = partial_out.shape[1] // tp_count
    pieces = lax.all_to_all(
        partial_out.reshape(req_count, tp_count, cols).transpose(1, 0, 2), "tp", 0, 0, tiled=True
    )
    return jnp.sum(pieces, axis=0).astype(jnp.bfloat16)


def solution(mesh):
    return jax.shard_map(
        on_device,
        mesh=mesh,
        in_specs=(
            P("seq", "tp"),
            P("seq", "tp"),
            P("seq", "tp"),
            P("seq", None, "tp"),
            P("seq", None, "tp"),
            P(None, "seq", "tp"),
            P(None, "seq", "tp"),
            P("seq"),
            P("seq"),
            P("seq"),
            P("seq"),
            P(),
            P(),
            P("tp"),
            P("tp"),
            P("tp", None),
        ),
        out_specs=P("seq", "tp"),
        check_vma=False,
    )
```

```python
import jax
import jax.numpy as jnp
from jax import lax
import functools

from jax.experimental import pallas as pl
from jax.sharding import Mesh, PartitionSpec as P

DH = 128
DV = 256
PG = 64


MASKED = -1e30


def _outbox_kernel(pick_ref, q_ref, kp_ref, vp_ref, lk_ref, lv_ref, colp_ref, coll_ref, place_ref,
                   ids_ref, out_ref, *, groups):
    qg = jnp.dot(pick_ref[...], q_ref[...], preferred_element_type=jnp.float32)
    row = lax.broadcasted_iota(jnp.int32, qg.shape, 0)
    lane = lax.broadcasted_iota(jnp.int32, qg.shape, 1)
    keep = (lane < DH) == (row < groups)
    qsel = jnp.where(keep, qg, 0.0).astype(jnp.bfloat16)
    dims = (((1,), (1,)), ((), ()))
    s_pool = lax.dot_general(qsel, kp_ref[...], dims, preferred_element_type=jnp.float32) * DH ** (-0.5)
    s_long = lax.dot_general(qsel, lk_ref[...], dims, preferred_element_type=jnp.float32) * DH ** (-0.5)
    own = lax.broadcasted_iota(jnp.int32, (2 * groups, 1), 0)
    own = jnp.where(own < groups, own, own - groups)
    mask_pool = own == colp_ref[...]
    mask_long = own == coll_ref[...]
    s_pool = jnp.where(mask_pool, s_pool, MASKED)
    s_long = jnp.where(mask_long, s_long, MASKED)
    m = jnp.maximum(jnp.max(s_pool, axis=1, keepdims=True), jnp.max(s_long, axis=1, keepdims=True))
    w_pool = jnp.where(mask_pool, jnp.exp(s_pool - m), 0.0)
    w_long = jnp.where(mask_long, jnp.exp(s_long - m), 0.0)
    total = jnp.sum(w_pool, axis=1, keepdims=True) + jnp.sum(w_long, axis=1, keepdims=True)
    num = jnp.dot(w_pool.astype(jnp.bfloat16), vp_ref[...], preferred_element_type=jnp.float32)
    num = num + jnp.dot(w_long.astype(jnp.bfloat16), lv_ref[...], preferred_element_type=jnp.float32)
    numb = num.astype(jnp.bfloat16)
    stats = (m[:groups], m[groups:], total[:groups], total[groups:])
    slane = lax.broadcasted_iota(jnp.int32, (groups, 128), 1)
    block = ids_ref[...]
    for k, x in enumerate(stats):
        hi = x.astype(jnp.bfloat16).astype(jnp.float32)
        rest = x - hi
        mid = rest.astype(jnp.bfloat16).astype(jnp.float32)
        lo = rest - mid
        for piece, value in enumerate((hi, mid, lo)):
            block = jnp.where(slane == piece * 4 + k, value, block)
    packed = jnp.concatenate(
        [numb[:groups], numb[groups:], block.astype(jnp.bfloat16)], axis=1
    )
    out_ref[...] = jnp.dot(place_ref[...], packed, preferred_element_type=jnp.float32).astype(out_ref.dtype)


def outbox_kernel(pick, q_all, kp, vp, lk, lv, colp, coll, place, ids, width, interpret=False):
    groups = place.shape[1]
    kern = functools.partial(_outbox_kernel, groups=groups)
    return pl.pallas_call(
        kern,
        out_shape=jax.ShapeDtypeStruct((place.shape[0], width), jnp.bfloat16),
        interpret=interpret,
    )(pick, q_all, kp, vp, lk, lv, colp, coll, place, ids)


def split_three(x):
    hi = lax.reduce_precision(x, exponent_bits=8, mantissa_bits=7)
    rest = x - hi
    mid = lax.reduce_precision(rest, exponent_bits=8, mantissa_bits=7)
    lo = rest - mid
    return jnp.concatenate([hi, mid, lo], axis=-1).astype(jnp.bfloat16)


def join_three(x):
    n = x.shape[-1] // 3
    x = x.astype(jnp.float32)
    return (x[..., :n] + x[..., n : 2 * n]) + x[..., 2 * n :]


def on_device(
    query,
    new_key,
    new_value,
    key_pool,
    value_pool,
    long_key,
    long_value,
    serve_table,
    serve_len,
    page_slot,
    page_offset,
    long_request,
    long_len,
    lambda_head,
    norm_gain,
    out_weight,
):
    req_count = query.shape[0]
    serve_count = serve_table.shape[0]
    long_count = long_request.shape[0]
    seq_index = lax.axis_index(SEQ)
    y_count = lax.axis_size("y")
    near_count = lax.axis_size("x") * lax.axis_size("c")
    seq_count = y_count * near_count
    tp_count = lax.axis_size("z")
    all_queries = lax.all_to_all(
        jnp.broadcast_to(query[None], (seq_count,) + query.shape), SEQ, 0, 0, tiled=True
    )
    all_queries = all_queries.reshape(-1, 2 * DH)
    total = seq_count * req_count
    pool_count = key_pool.shape[0]
    cell_count = key_pool.shape[1]
    long_cells = long_key.shape[1]
    groups = 16
    width = 2 * DV + 128
    safe_slot = jnp.maximum(page_slot, 0)
    cell_pos = page_offset[:, None] + jnp.arange(cell_count)[None, :]
    live = (page_slot[:, None] >= 0) & (cell_pos < serve_len[safe_slot][:, None])
    pool_group = jnp.where(live, page_slot[:, None], -1).reshape(1, -1)
    long_pos = seq_index * long_cells + jnp.arange(long_cells)
    long_live = long_pos[None, :] < long_len[:, None]
    long_group = jnp.where(long_live, serve_count + jnp.arange(long_count)[:, None], -1).reshape(1, -1)
    row_req = jnp.concatenate([serve_table, long_request], axis=0)
    row_req = jnp.concatenate([row_req, jnp.full((groups - row_req.shape[0],), -1, row_req.dtype)])
    pick = (jnp.tile(jnp.maximum(row_req, 0), 2)[:, None] == jnp.arange(total)[None, :])
    per_y = total // y_count
    dest_y = jnp.where(row_req >= 0, row_req // per_y, -1)
    hit = (dest_y[None, :] == jnp.arange(y_count)[:, None])[:, :, None] & jnp.eye(groups, dtype=bool)[None]
    hit = hit.reshape(y_count * groups, groups)
    place = hit.at[:, groups - 1].set(jnp.logical_not(jnp.any(hit, axis=1)))
    id_hi = jnp.floor_divide(row_req, 32) * 32
    id_lo = row_req - id_hi
    lane = jnp.arange(128)[None, :]
    ids = jnp.where(lane == 12, id_hi[:, None], jnp.where(lane == 13, id_lo[:, None], 0)).astype(jnp.float32)
    outbox = outbox_kernel(
        pick.astype(jnp.bfloat16),
        all_queries,
        key_pool.reshape(pool_count * cell_count, -1),
        value_pool.reshape(pool_count * cell_count, -1),
        long_key.reshape(long_count * long_cells, -1),
        long_value.reshape(long_count * long_cells, -1),
        pool_group.astype(jnp.int32),
        long_group.astype(jnp.int32),
        place.astype(jnp.bfloat16),
        ids,
        width,
    )
    hop = lax.all_to_all(outbox.reshape(y_count, groups, width), "y", 0, 0, tiled=True)
    hop = hop.reshape(y_count * groups, width).astype(jnp.float32)
    hop_num = hop[:, : 2 * DV].reshape(-1, 2, DV)
    hop_stats = join_three(hop[:, 2 * DV : 2 * DV + 12])
    hop_req = (hop[:, 2 * DV + 12] + hop[:, 2 * DV + 13]).astype(jnp.int32)
    merged_rows = near_count * req_count
    member = (hop_req[None, :] >= 0) & (hop_req[None, :] % merged_rows == jnp.arange(merged_rows)[:, None])
    member = member[:, :, None]
    hop_max = hop_stats[:, 0:2]
    merged_max = jnp.max(jnp.where(member, hop_max[None], MASKED), axis=1)
    scale = jnp.where(member, jnp.exp(jnp.where(member, hop_max[None] - merged_max[:, None], 0.0)), 0.0)
    merged_sum = jnp.einsum("tkj,kj->tj", scale, hop_stats[:, 2:4], precision=lax.Precision.HIGHEST)
    merged_num = jnp.einsum("tkj,kjv->tjv", scale, hop_num, precision=lax.Precision.HIGHEST)
    pieces = split_three(jnp.concatenate([merged_max, merged_sum], axis=1))
    second = jnp.concatenate(
        [
            merged_num.reshape(merged_rows, 2 * DV).astype(jnp.bfloat16),
            pieces,
            jnp.zeros((merged_rows, width - 2 * DV - pieces.shape[1]), jnp.bfloat16),
        ],
        axis=1,
    )
    inbox = lax.all_to_all(
        second.reshape(near_count, req_count, width), ("x", "c"), 0, 0, tiled=True
    )
    sources = inbox.shape[0]
    in_num = inbox[:, :, : 2 * DV].astype(jnp.float32).reshape(sources, req_count, 2, DV)
    in_stats = join_three(inbox[:, :, 2 * DV : 2 * DV + 12])
    in_max = in_stats[:, :, 0:2]
    in_sum = in_stats[:, :, 2:4]
    own_queries = query.reshape(req_count, 2, DH)
    own_keys = new_key.reshape(req_count, 2, DH)
    own_scores = jnp.einsum(
        "rjd,rjd->rj", own_queries, own_keys, preferred_element_type=jnp.float32
    ) * DH ** (-0.5)
    best = jnp.maximum(own_scores, jnp.max(in_max, axis=0))
    factor = jnp.exp(in_max - best[None])
    own_weight = jnp.exp(own_scores - best)
    denom = own_weight + jnp.sum(factor * in_sum, axis=0)
    numer = own_weight[..., None] * new_value.reshape(req_count, 1, DV).astype(jnp.float32)
    numer = numer + jnp.sum(factor[..., None] * in_num, axis=0)
    attn = numer / denom[..., None]
    diff = attn[:, 0] - lambda_head[0] * attn[:, 1]
    normed = (
        diff
        * lax.rsqrt(jnp.mean(diff * diff, axis=-1, keepdims=True) + 1e-05)
        * norm_gain.reshape(1, DV)
    )
    normed = normed.astype(jnp.bfloat16)
    partial_out = jnp.dot(normed, out_weight, preferred_element_type=jnp.float32)
    cols = partial_out.shape[1] // tp_count
    pieces = lax.all_to_all(
        partial_out.reshape(req_count, tp_count, cols).transpose(1, 0, 2), "z", 0, 0, tiled=True
    )
    return jnp.sum(pieces, axis=0).astype(jnp.bfloat16)


SEQ = ("y", "x", "c")


def solution(mesh):
    y_count = mesh.shape["seq"] // 8
    parts = Mesh(mesh.devices.reshape(y_count, 4, 2, mesh.shape["tp"]), ("y", "x", "c", "z"))
    rows = P(SEQ, "z")
    pages = P(SEQ, None, "z")
    return jax.shard_map(
        on_device,
        mesh=parts,
        in_specs=(
            rows,
            rows,
            rows,
            pages,
            pages,
            P(None, SEQ, "z"),
            P(None, SEQ, "z"),
            P(SEQ),
            P(SEQ),
            P(SEQ),
            P(SEQ),
            P(),
            P(),
            P("z"),
            P("z"),
            P("z", None),
        ),
        out_specs=rows,
        check_vma=False,
    )
```

```python
import jax
import jax.numpy as jnp
from jax import lax
import functools

from jax.experimental import pallas as pl
from jax.sharding import Mesh, PartitionSpec as P

DH = 128
DV = 256
PG = 64


MASKED = -1e30


def _outbox_kernel(pick_ref, q_ref, kp_ref, vp_ref, lk_ref, lv_ref, colp_ref, coll_ref, place_ref,
                   ids_ref, out_ref, *, groups):
    qg = jnp.dot(pick_ref[...], q_ref[...], preferred_element_type=jnp.float32)
    row = lax.broadcasted_iota(jnp.int32, qg.shape, 0)
    lane = lax.broadcasted_iota(jnp.int32, qg.shape, 1)
    keep = (lane < DH) == (row < groups)
    qsel = jnp.where(keep, qg, 0.0).astype(jnp.bfloat16)
    dims = (((1,), (1,)), ((), ()))
    s_pool = lax.dot_general(qsel, kp_ref[...], dims, preferred_element_type=jnp.float32) * DH ** (-0.5)
    s_long = lax.dot_general(qsel, lk_ref[...], dims, preferred_element_type=jnp.float32) * DH ** (-0.5)
    own = lax.broadcasted_iota(jnp.int32, (2 * groups, 1), 0)
    own = jnp.where(own < groups, own, own - groups)
    mask_pool = own == colp_ref[...]
    mask_long = own == coll_ref[...]
    s_pool = jnp.where(mask_pool, s_pool, MASKED)
    s_long = jnp.where(mask_long, s_long, MASKED)
    m = jnp.maximum(jnp.max(s_pool, axis=1, keepdims=True), jnp.max(s_long, axis=1, keepdims=True))
    w_pool = jnp.where(mask_pool, jnp.exp(s_pool - m), 0.0)
    w_long = jnp.where(mask_long, jnp.exp(s_long - m), 0.0)
    total = jnp.sum(w_pool, axis=1, keepdims=True) + jnp.sum(w_long, axis=1, keepdims=True)
    num = jnp.dot(w_pool.astype(jnp.bfloat16), vp_ref[...], preferred_element_type=jnp.float32)
    num = num + jnp.dot(w_long.astype(jnp.bfloat16), lv_ref[...], preferred_element_type=jnp.float32)
    numb = num.astype(jnp.bfloat16)
    stats = (m[:groups], m[groups:], total[:groups], total[groups:])
    slane = lax.broadcasted_iota(jnp.int32, (groups, 128), 1)
    block = ids_ref[...]
    for k, x in enumerate(stats):
        hi = x.astype(jnp.bfloat16).astype(jnp.float32)
        rest = x - hi
        mid = rest.astype(jnp.bfloat16).astype(jnp.float32)
        lo = rest - mid
        for piece, value in enumerate((hi, mid, lo)):
            block = jnp.where(slane == piece * 4 + k, value, block)
    packed = jnp.concatenate(
        [numb[:groups], numb[groups:], block.astype(jnp.bfloat16)], axis=1
    )
    out_ref[...] = jnp.dot(place_ref[...], packed, preferred_element_type=jnp.float32).astype(out_ref.dtype)


def outbox_kernel(pick, q_all, kp, vp, lk, lv, colp, coll, place, ids, width, interpret=False):
    groups = place.shape[1]
    kern = functools.partial(_outbox_kernel, groups=groups)
    return pl.pallas_call(
        kern,
        out_shape=jax.ShapeDtypeStruct((place.shape[0], width), jnp.bfloat16),
        interpret=interpret,
    )(pick, q_all, kp, vp, lk, lv, colp, coll, place, ids)


def split_three(x):
    hi = lax.reduce_precision(x, exponent_bits=8, mantissa_bits=7)
    rest = x - hi
    mid = lax.reduce_precision(rest, exponent_bits=8, mantissa_bits=7)
    lo = rest - mid
    return jnp.concatenate([hi, mid, lo], axis=-1).astype(jnp.bfloat16)


def join_three(x):
    n = x.shape[-1] // 3
    x = x.astype(jnp.float32)
    return (x[..., :n] + x[..., n : 2 * n]) + x[..., 2 * n :]


def on_device(
    query,
    new_key,
    new_value,
    key_pool,
    value_pool,
    long_key,
    long_value,
    serve_table,
    serve_len,
    page_slot,
    page_offset,
    long_request,
    long_len,
    lambda_head,
    norm_gain,
    out_weight,
):
    req_count = query.shape[0]
    serve_count = serve_table.shape[0]
    long_count = long_request.shape[0]
    seq_index = lax.axis_index(SEQ)
    y_count = lax.axis_size("y")
    near_count = lax.axis_size("x") * lax.axis_size("c")
    seq_count = y_count * near_count
    tp_count = lax.axis_size("z")
    all_queries = lax.all_to_all(
        jnp.broadcast_to(query[None], (seq_count,) + query.shape), SEQ, 0, 0, tiled=True
    )
    all_queries = all_queries.reshape(-1, 2 * DH)
    total = seq_count * req_count
    pool_count = key_pool.shape[0]
    cell_count = key_pool.shape[1]
    long_cells = long_key.shape[1]
    groups = 16
    width = 2 * DV + 128
    safe_slot = jnp.maximum(page_slot, 0)
    cell_pos = page_offset[:, None] + jnp.arange(cell_count)[None, :]
    live = (page_slot[:, None] >= 0) & (cell_pos < serve_len[safe_slot][:, None])
    pool_group = jnp.where(live, page_slot[:, None], -1).reshape(1, -1)
    long_pos = seq_index * long_cells + jnp.arange(long_cells)
    long_live = long_pos[None, :] < long_len[:, None]
    long_group = jnp.where(long_live, serve_count + jnp.arange(long_count)[:, None], -1).reshape(1, -1)
    row_req = jnp.concatenate([serve_table, long_request], axis=0)
    row_req = jnp.concatenate([row_req, jnp.full((groups - row_req.shape[0],), -1, row_req.dtype)])
    pick = (jnp.tile(jnp.maximum(row_req, 0), 2)[:, None] == jnp.arange(total)[None, :])
    dest_near = jnp.where(row_req >= 0, (row_req // req_count) % near_count, -1)
    hit = (dest_near[None, :] == jnp.arange(near_count)[:, None])[:, :, None] & jnp.eye(groups, dtype=bool)[None]
    hit = hit.reshape(near_count * groups, groups)
    place = hit.at[:, groups - 1].set(jnp.logical_not(jnp.any(hit, axis=1)))
    id_hi = jnp.floor_divide(row_req, 32) * 32
    id_lo = row_req - id_hi
    lane = jnp.arange(128)[None, :]
    ids = jnp.where(lane == 12, id_hi[:, None], jnp.where(lane == 13, id_lo[:, None], 0)).astype(jnp.float32)
    outbox = outbox_kernel(
        pick.astype(jnp.bfloat16),
        all_queries,
        key_pool.reshape(pool_count * cell_count, -1),
        value_pool.reshape(pool_count * cell_count, -1),
        long_key.reshape(long_count * long_cells, -1),
        long_value.reshape(long_count * long_cells, -1),
        pool_group.astype(jnp.int32),
        long_group.astype(jnp.int32),
        place.astype(jnp.bfloat16),
        ids,
        width,
    )
    hop = lax.all_to_all(outbox.reshape(near_count, groups, width), ("x", "c"), 0, 0, tiled=True)
    hop = hop.reshape(near_count * groups, width).astype(jnp.float32)
    hop_num = hop[:, : 2 * DV].reshape(-1, 2, DV)
    hop_stats = join_three(hop[:, 2 * DV : 2 * DV + 12])
    hop_req = (hop[:, 2 * DV + 12] + hop[:, 2 * DV + 13]).astype(jnp.int32)
    merged_rows = y_count * req_count
    merged_at = (hop_req // (near_count * req_count)) * req_count + hop_req % req_count
    member = (hop_req[None, :] >= 0) & (merged_at[None, :] == jnp.arange(merged_rows)[:, None])
    member = member[:, :, None]
    hop_max = hop_stats[:, 0:2]
    merged_max = jnp.max(jnp.where(member, hop_max[None], MASKED), axis=1)
    scale = jnp.where(member, jnp.exp(jnp.where(member, hop_max[None] - merged_max[:, None], 0.0)), 0.0)
    merged_sum = jnp.einsum("tkj,kj->tj", scale, hop_stats[:, 2:4], precision=lax.Precision.HIGHEST)
    merged_num = jnp.einsum("tkj,kjv->tjv", scale, hop_num, precision=lax.Precision.HIGHEST)
    pieces = split_three(jnp.concatenate([merged_max, merged_sum], axis=1))
    second = jnp.concatenate(
        [
            merged_num.reshape(merged_rows, 2 * DV).astype(jnp.bfloat16),
            pieces,
            jnp.zeros((merged_rows, width - 2 * DV - pieces.shape[1]), jnp.bfloat16),
        ],
        axis=1,
    )
    inbox = lax.all_to_all(
        second.reshape(y_count, req_count, width), "y", 0, 0, tiled=True
    )
    sources = inbox.shape[0]
    in_num = inbox[:, :, : 2 * DV].astype(jnp.float32).reshape(sources, req_count, 2, DV)
    in_stats = join_three(inbox[:, :, 2 * DV : 2 * DV + 12])
    in_max = in_stats[:, :, 0:2]
    in_sum = in_stats[:, :, 2:4]
    own_queries = query.reshape(req_count, 2, DH)
    own_keys = new_key.reshape(req_count, 2, DH)
    own_scores = jnp.einsum(
        "rjd,rjd->rj", own_queries, own_keys, preferred_element_type=jnp.float32
    ) * DH ** (-0.5)
    best = jnp.maximum(own_scores, jnp.max(in_max, axis=0))
    factor = jnp.exp(in_max - best[None])
    own_weight = jnp.exp(own_scores - best)
    denom = own_weight + jnp.sum(factor * in_sum, axis=0)
    numer = own_weight[..., None] * new_value.reshape(req_count, 1, DV).astype(jnp.float32)
    numer = numer + jnp.sum(factor[..., None] * in_num, axis=0)
    attn = numer / denom[..., None]
    diff = attn[:, 0] - lambda_head[0] * attn[:, 1]
    normed = (
        diff
        * lax.rsqrt(jnp.mean(diff * diff, axis=-1, keepdims=True) + 1e-05)
        * norm_gain.reshape(1, DV)
    )
    normed = normed.astype(jnp.bfloat16)
    partial_out = jnp.dot(normed, out_weight, preferred_element_type=jnp.float32)
    cols = partial_out.shape[1] // tp_count
    pieces = lax.all_to_all(
        partial_out.reshape(req_count, tp_count, cols).transpose(1, 0, 2), "z", 0, 0, tiled=True
    )
    return jnp.sum(pieces, axis=0).astype(jnp.bfloat16)


SEQ = ("y", "x", "c")


def solution(mesh):
    y_count = mesh.shape["seq"] // 8
    parts = Mesh(mesh.devices.reshape(y_count, 4, 2, mesh.shape["tp"]), ("y", "x", "c", "z"))
    rows = P(SEQ, "z")
    pages = P(SEQ, None, "z")
    return jax.shard_map(
        on_device,
        mesh=parts,
        in_specs=(
            rows,
            rows,
            rows,
            pages,
            pages,
            P(None, SEQ, "z"),
            P(None, SEQ, "z"),
            P(SEQ),
            P(SEQ),
            P(SEQ),
            P(SEQ),
            P(),
            P(),
            P("z"),
            P("z"),
            P("z", None),
        ),
        out_specs=rows,
        check_vma=False,
    )
```

```python
import jax
import jax.numpy as jnp
from jax import lax
import functools

from jax.experimental import pallas as pl
from jax.sharding import Mesh, PartitionSpec as P

DH = 128
DV = 256
PG = 64


MASKED = -1e30


def _outbox_kernel(pick_ref, q_ref, kp_ref, vp_ref, lk_ref, lv_ref, colp_ref, coll_ref, place_ref,
                   ids_ref, out_ref, *, groups):
    qg = jnp.dot(pick_ref[...], q_ref[...], preferred_element_type=jnp.float32)
    row = lax.broadcasted_iota(jnp.int32, qg.shape, 0)
    lane = lax.broadcasted_iota(jnp.int32, qg.shape, 1)
    keep = (lane < DH) == (row < groups)
    qsel = jnp.where(keep, qg, 0.0).astype(jnp.bfloat16)
    dims = (((1,), (1,)), ((), ()))
    s_pool = lax.dot_general(qsel, kp_ref[...], dims, preferred_element_type=jnp.float32) * DH ** (-0.5)
    s_long = lax.dot_general(qsel, lk_ref[...], dims, preferred_element_type=jnp.float32) * DH ** (-0.5)
    own = lax.broadcasted_iota(jnp.int32, (2 * groups, 1), 0)
    own = jnp.where(own < groups, own, own - groups)
    mask_pool = own == colp_ref[...]
    mask_long = own == coll_ref[...]
    s_pool = jnp.where(mask_pool, s_pool, MASKED)
    s_long = jnp.where(mask_long, s_long, MASKED)
    m = jnp.maximum(jnp.max(s_pool, axis=1, keepdims=True), jnp.max(s_long, axis=1, keepdims=True))
    w_pool = jnp.where(mask_pool, jnp.exp(s_pool - m), 0.0)
    w_long = jnp.where(mask_long, jnp.exp(s_long - m), 0.0)
    total = jnp.sum(w_pool, axis=1, keepdims=True) + jnp.sum(w_long, axis=1, keepdims=True)
    num = jnp.dot(w_pool.astype(jnp.bfloat16), vp_ref[...], preferred_element_type=jnp.float32)
    num = num + jnp.dot(w_long.astype(jnp.bfloat16), lv_ref[...], preferred_element_type=jnp.float32)
    numb = num.astype(jnp.bfloat16)
    stats = (m[:groups], m[groups:], total[:groups], total[groups:])
    slane = lax.broadcasted_iota(jnp.int32, (groups, 128), 1)
    block = ids_ref[...]
    for k, x in enumerate(stats):
        hi = x.astype(jnp.bfloat16).astype(jnp.float32)
        rest = x - hi
        mid = rest.astype(jnp.bfloat16).astype(jnp.float32)
        lo = rest - mid
        for piece, value in enumerate((hi, mid, lo)):
            block = jnp.where(slane == piece * 4 + k, value, block)
    packed = jnp.concatenate(
        [numb[:groups], numb[groups:], block.astype(jnp.bfloat16)], axis=1
    )
    out_ref[...] = jnp.dot(place_ref[...], packed, preferred_element_type=jnp.float32).astype(out_ref.dtype)


def outbox_kernel(pick, q_all, kp, vp, lk, lv, colp, coll, place, ids, width, interpret=False):
    groups = place.shape[1]
    kern = functools.partial(_outbox_kernel, groups=groups)
    return pl.pallas_call(
        kern,
        out_shape=jax.ShapeDtypeStruct((place.shape[0], width), jnp.bfloat16),
        interpret=interpret,
    )(pick, q_all, kp, vp, lk, lv, colp, coll, place, ids)


def split_three(x):
    hi = lax.reduce_precision(x, exponent_bits=8, mantissa_bits=7)
    rest = x - hi
    mid = lax.reduce_precision(rest, exponent_bits=8, mantissa_bits=7)
    lo = rest - mid
    return jnp.concatenate([hi, mid, lo], axis=-1).astype(jnp.bfloat16)


def join_three(x):
    n = x.shape[-1] // 3
    x = x.astype(jnp.float32)
    return (x[..., :n] + x[..., n : 2 * n]) + x[..., 2 * n :]


def on_device(
    query,
    new_key,
    new_value,
    key_pool,
    value_pool,
    long_key,
    long_value,
    serve_table,
    serve_len,
    page_slot,
    page_offset,
    long_request,
    long_len,
    lambda_head,
    norm_gain,
    out_weight,
):
    req_count = query.shape[0]
    serve_count = serve_table.shape[0]
    long_count = long_request.shape[0]
    seq_index = lax.axis_index(SEQ)
    y_count = lax.axis_size("y")
    near_count = lax.axis_size("x") * lax.axis_size("c")
    seq_count = y_count * near_count
    tp_count = lax.axis_size("z")
    near_queries = lax.all_to_all(
        jnp.broadcast_to(query[None], (near_count,) + query.shape), ("x", "c"), 0, 0, tiled=True
    ).reshape(1, near_count * req_count, -1)
    all_queries = lax.all_to_all(
        jnp.broadcast_to(near_queries, (y_count,) + near_queries.shape[1:]), "y", 0, 0, tiled=True
    )
    all_queries = all_queries.reshape(-1, 2 * DH)
    total = seq_count * req_count
    pool_count = key_pool.shape[0]
    cell_count = key_pool.shape[1]
    long_cells = long_key.shape[1]
    groups = 16
    width = 2 * DV + 128
    safe_slot = jnp.maximum(page_slot, 0)
    cell_pos = page_offset[:, None] + jnp.arange(cell_count)[None, :]
    live = (page_slot[:, None] >= 0) & (cell_pos < serve_len[safe_slot][:, None])
    pool_group = jnp.where(live, page_slot[:, None], -1).reshape(1, -1)
    long_pos = seq_index * long_cells + jnp.arange(long_cells)
    long_live = long_pos[None, :] < long_len[:, None]
    long_group = jnp.where(long_live, serve_count + jnp.arange(long_count)[:, None], -1).reshape(1, -1)
    row_req = jnp.concatenate([serve_table, long_request], axis=0)
    row_req = jnp.concatenate([row_req, jnp.full((groups - row_req.shape[0],), -1, row_req.dtype)])
    pick = (jnp.tile(jnp.maximum(row_req, 0), 2)[:, None] == jnp.arange(total)[None, :])
    dest_near = jnp.where(row_req >= 0, (row_req // req_count) % near_count, -1)
    hit = (dest_near[None, :] == jnp.arange(near_count)[:, None])[:, :, None] & jnp.eye(groups, dtype=bool)[None]
    hit = hit.reshape(near_count * groups, groups)
    place = hit.at[:, groups - 1].set(jnp.logical_not(jnp.any(hit, axis=1)))
    id_hi = jnp.floor_divide(row_req, 32) * 32
    id_lo = row_req - id_hi
    lane = jnp.arange(128)[None, :]
    ids = jnp.where(lane == 12, id_hi[:, None], jnp.where(lane == 13, id_lo[:, None], 0)).astype(jnp.float32)
    outbox = outbox_kernel(
        pick.astype(jnp.bfloat16),
        all_queries,
        key_pool.reshape(pool_count * cell_count, -1),
        value_pool.reshape(pool_count * cell_count, -1),
        long_key.reshape(long_count * long_cells, -1),
        long_value.reshape(long_count * long_cells, -1),
        pool_group.astype(jnp.int32),
        long_group.astype(jnp.int32),
        place.astype(jnp.bfloat16),
        ids,
        width,
    )
    hop = lax.all_to_all(outbox.reshape(near_count, groups, width), ("x", "c"), 0, 0, tiled=True)
    hop = hop.reshape(near_count * groups, width).astype(jnp.float32)
    hop_num = hop[:, : 2 * DV].reshape(-1, 2, DV)
    hop_stats = join_three(hop[:, 2 * DV : 2 * DV + 12])
    hop_req = (hop[:, 2 * DV + 12] + hop[:, 2 * DV + 13]).astype(jnp.int32)
    merged_rows = y_count * req_count
    merged_at = (hop_req // (near_count * req_count)) * req_count + hop_req % req_count
    member = (hop_req[None, :] >= 0) & (merged_at[None, :] == jnp.arange(merged_rows)[:, None])
    member = member[:, :, None]
    hop_max = hop_stats[:, 0:2]
    merged_max = jnp.max(jnp.where(member, hop_max[None], MASKED), axis=1)
    scale = jnp.where(member, jnp.exp(jnp.where(member, hop_max[None] - merged_max[:, None], 0.0)), 0.0)
    merged_sum = jnp.einsum("tkj,kj->tj", scale, hop_stats[:, 2:4], precision=lax.Precision.HIGHEST)
    merged_num = jnp.einsum("tkj,kjv->tjv", scale, hop_num, precision=lax.Precision.HIGHEST)
    pieces = split_three(jnp.concatenate([merged_max, merged_sum], axis=1))
    second = jnp.concatenate(
        [
            merged_num.reshape(merged_rows, 2 * DV).astype(jnp.bfloat16),
            pieces,
            jnp.zeros((merged_rows, width - 2 * DV - pieces.shape[1]), jnp.bfloat16),
        ],
        axis=1,
    )
    inbox = lax.all_to_all(
        second.reshape(y_count, req_count, width), "y", 0, 0, tiled=True
    )
    sources = inbox.shape[0]
    in_num = inbox[:, :, : 2 * DV].astype(jnp.float32).reshape(sources, req_count, 2, DV)
    in_stats = join_three(inbox[:, :, 2 * DV : 2 * DV + 12])
    in_max = in_stats[:, :, 0:2]
    in_sum = in_stats[:, :, 2:4]
    own_queries = query.reshape(req_count, 2, DH)
    own_keys = new_key.reshape(req_count, 2, DH)
    own_scores = jnp.einsum(
        "rjd,rjd->rj", own_queries, own_keys, preferred_element_type=jnp.float32
    ) * DH ** (-0.5)
    best = jnp.maximum(own_scores, jnp.max(in_max, axis=0))
    factor = jnp.exp(in_max - best[None])
    own_weight = jnp.exp(own_scores - best)
    denom = own_weight + jnp.sum(factor * in_sum, axis=0)
    numer = own_weight[..., None] * new_value.reshape(req_count, 1, DV).astype(jnp.float32)
    numer = numer + jnp.sum(factor[..., None] * in_num, axis=0)
    attn = numer / denom[..., None]
    diff = attn[:, 0] - lambda_head[0] * attn[:, 1]
    normed = (
        diff
        * lax.rsqrt(jnp.mean(diff * diff, axis=-1, keepdims=True) + 1e-05)
        * norm_gain.reshape(1, DV)
    )
    normed = normed.astype(jnp.bfloat16)
    partial_out = jnp.dot(normed, out_weight, preferred_element_type=jnp.float32)
    cols = partial_out.shape[1] // tp_count
    pieces = lax.all_to_all(
        partial_out.reshape(req_count, tp_count, cols).transpose(1, 0, 2), "z", 0, 0, tiled=True
    )
    return jnp.sum(pieces, axis=0).astype(jnp.bfloat16)


SEQ = ("y", "x", "c")


def solution(mesh):
    y_count = mesh.shape["seq"] // 8
    parts = Mesh(mesh.devices.reshape(y_count, 4, 2, mesh.shape["tp"]), ("y", "x", "c", "z"))
    rows = P(SEQ, "z")
    pages = P(SEQ, None, "z")
    return jax.shard_map(
        on_device,
        mesh=parts,
        in_specs=(
            rows,
            rows,
            rows,
            pages,
            pages,
            P(None, SEQ, "z"),
            P(None, SEQ, "z"),
            P(SEQ),
            P(SEQ),
            P(SEQ),
            P(SEQ),
            P(),
            P(),
            P("z"),
            P("z"),
            P("z", None),
        ),
        out_specs=rows,
        check_vma=False,
    )
```

```python
import jax
import jax.numpy as jnp
from jax import lax
import functools

from jax.experimental import pallas as pl
from jax.sharding import Mesh, PartitionSpec as P

DH = 128
DV = 256
PG = 64


MASKED = -1e30


def _outbox_kernel(rr_ref, q_ref, kp_ref, vp_ref, lk_ref, lv_ref, colp_ref, coll_ref,
                   out_ref, *, groups, req_shift, near):
    rr = rr_ref[...]
    rr2 = jnp.concatenate([rr, rr], axis=0)
    total = q_ref.shape[0]
    qlane = lax.broadcasted_iota(jnp.int32, (2 * groups, total), 1)
    pick = (qlane == jnp.maximum(rr2, 0)).astype(jnp.bfloat16)
    qg = jnp.dot(pick, q_ref[...], preferred_element_type=jnp.float32)
    row = lax.broadcasted_iota(jnp.int32, qg.shape, 0)
    lane = lax.broadcasted_iota(jnp.int32, qg.shape, 1)
    keep = (lane < DH) == (row < groups)
    qsel = jnp.where(keep, qg, 0.0).astype(jnp.bfloat16)
    dims = (((1,), (1,)), ((), ()))
    s_pool = lax.dot_general(qsel, kp_ref[...], dims, preferred_element_type=jnp.float32) * DH ** (-0.5)
    s_long = lax.dot_general(qsel, lk_ref[...], dims, preferred_element_type=jnp.float32) * DH ** (-0.5)
    own = lax.broadcasted_iota(jnp.int32, (2 * groups, 1), 0)
    own = jnp.where(own < groups, own, own - groups)
    mask_pool = own == colp_ref[...]
    mask_long = own == coll_ref[...]
    s_pool = jnp.where(mask_pool, s_pool, MASKED)
    s_long = jnp.where(mask_long, s_long, MASKED)
    m = jnp.maximum(jnp.max(s_pool, axis=1, keepdims=True), jnp.max(s_long, axis=1, keepdims=True))
    w_pool = jnp.where(mask_pool, jnp.exp(s_pool - m), 0.0)
    w_long = jnp.where(mask_long, jnp.exp(s_long - m), 0.0)
    total = jnp.sum(w_pool, axis=1, keepdims=True) + jnp.sum(w_long, axis=1, keepdims=True)
    num = jnp.dot(w_pool.astype(jnp.bfloat16), vp_ref[...], preferred_element_type=jnp.float32)
    num = num + jnp.dot(w_long.astype(jnp.bfloat16), lv_ref[...], preferred_element_type=jnp.float32)
    numb = num.astype(jnp.bfloat16)
    stats = (m[:groups], m[groups:], total[:groups], total[groups:])
    slane = lax.broadcasted_iota(jnp.int32, (groups, 128), 1)
    id_hi = lax.shift_left(lax.shift_right_arithmetic(rr, 5), 5)
    id_lo = rr - id_hi
    block = jnp.where(
        slane == 12, id_hi.astype(jnp.float32), jnp.where(slane == 13, id_lo.astype(jnp.float32), 0.0)
    )
    for k, x in enumerate(stats):
        hi = x.astype(jnp.bfloat16).astype(jnp.float32)
        rest = x - hi
        mid = rest.astype(jnp.bfloat16).astype(jnp.float32)
        lo = rest - mid
        for piece, value in enumerate((hi, mid, lo)):
            block = jnp.where(slane == piece * 4 + k, value, block)
    packed = jnp.concatenate(
        [numb[:groups], numb[groups:], block.astype(jnp.bfloat16)], axis=1
    )
    rrb = jnp.concatenate([rr] * near, axis=0)
    prow = lax.broadcasted_iota(jnp.int32, rrb.shape, 0)
    slot = prow % groups
    dest = jnp.where(rrb >= 0, lax.shift_right_logical(rrb, req_shift) % near, -1)
    hit = dest == prow // groups
    glane = lax.broadcasted_iota(jnp.int32, (near * groups, groups), 1)
    place = ((glane == slot) & hit) | ((glane == groups - 1) & jnp.logical_not(hit))
    out_ref[...] = jnp.dot(
        place.astype(jnp.bfloat16), packed, preferred_element_type=jnp.float32
    ).astype(out_ref.dtype)


def outbox_kernel(rr, q_all, kp, vp, lk, lv, colp, coll, near, req_count, width, interpret=False):
    groups = rr.shape[0]
    req_shift = req_count.bit_length() - 1
    assert req_count == 1 << req_shift
    kern = functools.partial(_outbox_kernel, groups=groups, req_shift=req_shift, near=near)
    return pl.pallas_call(
        kern,
        out_shape=jax.ShapeDtypeStruct((near * groups, width), jnp.bfloat16),
        interpret=interpret,
    )(rr, q_all, kp, vp, lk, lv, colp, coll)


def split_three(x):
    hi = lax.reduce_precision(x, exponent_bits=8, mantissa_bits=7)
    rest = x - hi
    mid = lax.reduce_precision(rest, exponent_bits=8, mantissa_bits=7)
    lo = rest - mid
    return jnp.concatenate([hi, mid, lo], axis=-1).astype(jnp.bfloat16)


def join_three(x):
    n = x.shape[-1] // 3
    x = x.astype(jnp.float32)
    return (x[..., :n] + x[..., n : 2 * n]) + x[..., 2 * n :]


def on_device(
    query,
    new_key,
    new_value,
    key_pool,
    value_pool,
    long_key,
    long_value,
    serve_table,
    serve_len,
    page_slot,
    page_offset,
    long_request,
    long_len,
    lambda_head,
    norm_gain,
    out_weight,
):
    req_count = query.shape[0]
    serve_count = serve_table.shape[0]
    long_count = long_request.shape[0]
    seq_index = lax.axis_index(SEQ)
    y_count = lax.axis_size("y")
    near_count = lax.axis_size("x") * lax.axis_size("c")
    seq_count = y_count * near_count
    tp_count = lax.axis_size("z")
    all_queries = lax.all_to_all(
        jnp.broadcast_to(query[None], (seq_count,) + query.shape), SEQ, 0, 0, tiled=True
    )
    all_queries = all_queries.reshape(-1, 2 * DH)
    total = seq_count * req_count
    pool_count = key_pool.shape[0]
    cell_count = key_pool.shape[1]
    long_cells = long_key.shape[1]
    groups = 16
    width = 2 * DV + 128
    safe_slot = jnp.maximum(page_slot, 0)
    cell_pos = page_offset[:, None] + jnp.arange(cell_count)[None, :]
    live = (page_slot[:, None] >= 0) & (cell_pos < serve_len[safe_slot][:, None])
    pool_group = jnp.where(live, page_slot[:, None], -1).reshape(1, -1)
    long_pos = seq_index * long_cells + jnp.arange(long_cells)
    long_live = long_pos[None, :] < long_len[:, None]
    long_group = jnp.where(long_live, serve_count + jnp.arange(long_count)[:, None], -1).reshape(1, -1)
    row_req = jnp.concatenate([serve_table, long_request], axis=0)
    row_req = jnp.concatenate([row_req, jnp.full((groups - row_req.shape[0],), -1, row_req.dtype)])
    outbox = outbox_kernel(
        row_req.reshape(groups, 1).astype(jnp.int32),
        all_queries,
        key_pool.reshape(pool_count * cell_count, -1),
        value_pool.reshape(pool_count * cell_count, -1),
        long_key.reshape(long_count * long_cells, -1),
        long_value.reshape(long_count * long_cells, -1),
        pool_group.astype(jnp.int32),
        long_group.astype(jnp.int32),
        near_count,
        req_count,
        width,
    )
    hop = lax.all_to_all(outbox.reshape(near_count, groups, width), ("x", "c"), 0, 0, tiled=True)
    hop = hop.reshape(near_count * groups, width).astype(jnp.float32)
    hop_num = hop[:, : 2 * DV].reshape(-1, 2, DV)
    hop_stats = join_three(hop[:, 2 * DV : 2 * DV + 12])
    hop_req = (hop[:, 2 * DV + 12] + hop[:, 2 * DV + 13]).astype(jnp.int32)
    merged_rows = y_count * req_count
    merged_at = (hop_req // (near_count * req_count)) * req_count + hop_req % req_count
    member = (hop_req[None, :] >= 0) & (merged_at[None, :] == jnp.arange(merged_rows)[:, None])
    member = member[:, :, None]
    hop_max = hop_stats[:, 0:2]
    merged_max = jnp.max(jnp.where(member, hop_max[None], MASKED), axis=1)
    scale = jnp.where(member, jnp.exp(jnp.where(member, hop_max[None] - merged_max[:, None], 0.0)), 0.0)
    merged_sum = jnp.einsum("tkj,kj->tj", scale, hop_stats[:, 2:4], precision=lax.Precision.HIGHEST)
    merged_num = jnp.einsum("tkj,kjv->tjv", scale, hop_num, precision=lax.Precision.HIGHEST)
    pieces = split_three(jnp.concatenate([merged_max, merged_sum], axis=1))
    second = jnp.concatenate(
        [
            merged_num.reshape(merged_rows, 2 * DV).astype(jnp.bfloat16),
            pieces,
            jnp.zeros((merged_rows, width - 2 * DV - pieces.shape[1]), jnp.bfloat16),
        ],
        axis=1,
    )
    inbox = lax.all_to_all(
        second.reshape(y_count, req_count, width), "y", 0, 0, tiled=True
    )
    sources = inbox.shape[0]
    in_num = inbox[:, :, : 2 * DV].astype(jnp.float32).reshape(sources, req_count, 2, DV)
    in_stats = join_three(inbox[:, :, 2 * DV : 2 * DV + 12])
    in_max = in_stats[:, :, 0:2]
    in_sum = in_stats[:, :, 2:4]
    own_queries = query.reshape(req_count, 2, DH)
    own_keys = new_key.reshape(req_count, 2, DH)
    own_scores = jnp.einsum(
        "rjd,rjd->rj", own_queries, own_keys, preferred_element_type=jnp.float32
    ) * DH ** (-0.5)
    best = jnp.maximum(own_scores, jnp.max(in_max, axis=0))
    factor = jnp.exp(in_max - best[None])
    own_weight = jnp.exp(own_scores - best)
    denom = own_weight + jnp.sum(factor * in_sum, axis=0)
    numer = own_weight[..., None] * new_value.reshape(req_count, 1, DV).astype(jnp.float32)
    numer = numer + jnp.sum(factor[..., None] * in_num, axis=0)
    attn = numer / denom[..., None]
    diff = attn[:, 0] - lambda_head[0] * attn[:, 1]
    normed = (
        diff
        * lax.rsqrt(jnp.mean(diff * diff, axis=-1, keepdims=True) + 1e-05)
        * norm_gain.reshape(1, DV)
    )
    normed = normed.astype(jnp.bfloat16)
    partial_out = jnp.dot(normed, out_weight, preferred_element_type=jnp.float32)
    cols = partial_out.shape[1] // tp_count
    pieces = lax.all_to_all(
        partial_out.reshape(req_count, tp_count, cols).transpose(1, 0, 2), "z", 0, 0, tiled=True
    )
    return jnp.sum(pieces, axis=0).astype(jnp.bfloat16)


SEQ = ("y", "x", "c")


def solution(mesh):
    y_count = mesh.shape["seq"] // 8
    parts = Mesh(mesh.devices.reshape(y_count, 4, 2, mesh.shape["tp"]), ("y", "x", "c", "z"))
    rows = P(SEQ, "z")
    pages = P(SEQ, None, "z")
    return jax.shard_map(
        on_device,
        mesh=parts,
        in_specs=(
            rows,
            rows,
            rows,
            pages,
            pages,
            P(None, SEQ, "z"),
            P(None, SEQ, "z"),
            P(SEQ),
            P(SEQ),
            P(SEQ),
            P(SEQ),
            P(),
            P(),
            P("z"),
            P("z"),
            P("z", None),
        ),
        out_specs=rows,
        check_vma=False,
    )
```

```python
import jax
import jax.numpy as jnp
from jax import lax
import functools

from jax.experimental import pallas as pl
from jax.sharding import Mesh, PartitionSpec as P

DH = 128
DV = 256
PG = 64


MASKED = -1e30


def _outbox_kernel(rr_ref, q_ref, kp_ref, vp_ref, lk_ref, lv_ref, colp_ref, coll_ref,
                   out_ref, *, groups, req_shift, near):
    rr = rr_ref[...]
    rr2 = jnp.concatenate([rr, rr], axis=0)
    total = q_ref.shape[0]
    qlane = lax.broadcasted_iota(jnp.int32, (2 * groups, total), 1)
    pick = (qlane == jnp.maximum(rr2, 0)).astype(jnp.bfloat16)
    qg = jnp.dot(pick, q_ref[...], preferred_element_type=jnp.float32)
    row = lax.broadcasted_iota(jnp.int32, qg.shape, 0)
    lane = lax.broadcasted_iota(jnp.int32, qg.shape, 1)
    keep = (lane < DH) == (row < groups)
    qsel = jnp.where(keep, qg, 0.0).astype(jnp.bfloat16)
    dims = (((1,), (1,)), ((), ()))
    s_pool = lax.dot_general(qsel, kp_ref[...], dims, preferred_element_type=jnp.float32) * DH ** (-0.5)
    s_long = lax.dot_general(qsel, lk_ref[...], dims, preferred_element_type=jnp.float32) * DH ** (-0.5)
    own = lax.broadcasted_iota(jnp.int32, (2 * groups, 1), 0)
    own = jnp.where(own < groups, own, own - groups)
    mask_pool = own == colp_ref[...]
    mask_long = own == coll_ref[...]
    s_pool = jnp.where(mask_pool, s_pool, MASKED)
    s_long = jnp.where(mask_long, s_long, MASKED)
    m = jnp.maximum(jnp.max(s_pool, axis=1, keepdims=True), jnp.max(s_long, axis=1, keepdims=True))
    w_pool = jnp.where(mask_pool, jnp.exp(s_pool - m), 0.0)
    w_long = jnp.where(mask_long, jnp.exp(s_long - m), 0.0)
    total = jnp.sum(w_pool, axis=1, keepdims=True) + jnp.sum(w_long, axis=1, keepdims=True)
    num = jnp.dot(w_pool.astype(jnp.bfloat16), vp_ref[...], preferred_element_type=jnp.float32)
    num = num + jnp.dot(w_long.astype(jnp.bfloat16), lv_ref[...], preferred_element_type=jnp.float32)
    numb = num.astype(jnp.bfloat16)
    stats = (m[:groups], m[groups:], total[:groups], total[groups:])
    slane = lax.broadcasted_iota(jnp.int32, (groups, 128), 1)
    id_hi = lax.shift_left(lax.shift_right_arithmetic(rr, 5), 5)
    id_lo = rr - id_hi
    block = jnp.where(
        slane == 12, id_hi.astype(jnp.float32), jnp.where(slane == 13, id_lo.astype(jnp.float32), 0.0)
    )
    for k, x in enumerate(stats):
        hi = x.astype(jnp.bfloat16).astype(jnp.float32)
        rest = x - hi
        mid = rest.astype(jnp.bfloat16).astype(jnp.float32)
        lo = rest - mid
        for piece, value in enumerate((hi, mid, lo)):
            block = jnp.where(slane == piece * 4 + k, value, block)
    packed = jnp.concatenate(
        [numb[:groups], numb[groups:], block.astype(jnp.bfloat16)], axis=1
    )
    rrb = jnp.concatenate([rr] * near, axis=0)
    prow = lax.broadcasted_iota(jnp.int32, rrb.shape, 0)
    slot = prow % groups
    dest = jnp.where(rrb >= 0, lax.shift_right_logical(rrb, req_shift) % near, -1)
    hit = dest == prow // groups
    glane = lax.broadcasted_iota(jnp.int32, (near * groups, groups), 1)
    place = ((glane == slot) & hit) | ((glane == groups - 1) & jnp.logical_not(hit))
    out_ref[...] = jnp.dot(
        place.astype(jnp.bfloat16), packed, preferred_element_type=jnp.float32
    ).astype(out_ref.dtype)


def outbox_kernel(rr, q_all, kp, vp, lk, lv, colp, coll, near, req_count, width, interpret=False):
    groups = rr.shape[0]
    req_shift = req_count.bit_length() - 1
    assert req_count == 1 << req_shift
    kern = functools.partial(_outbox_kernel, groups=groups, req_shift=req_shift, near=near)
    return pl.pallas_call(
        kern,
        out_shape=jax.ShapeDtypeStruct((near * groups, width), jnp.bfloat16),
        interpret=interpret,
    )(rr, q_all, kp, vp, lk, lv, colp, coll)


def split_three(x):
    hi = lax.reduce_precision(x, exponent_bits=8, mantissa_bits=7)
    rest = x - hi
    mid = lax.reduce_precision(rest, exponent_bits=8, mantissa_bits=7)
    lo = rest - mid
    return jnp.concatenate([hi, mid, lo], axis=-1).astype(jnp.bfloat16)


def join_three(x):
    n = x.shape[-1] // 3
    x = x.astype(jnp.float32)
    return (x[..., :n] + x[..., n : 2 * n]) + x[..., 2 * n :]


def on_device(
    query,
    new_key,
    new_value,
    key_pool,
    value_pool,
    long_key,
    long_value,
    serve_table,
    serve_len,
    page_slot,
    page_offset,
    long_request,
    long_len,
    lambda_head,
    norm_gain,
    out_weight,
):
    req_count = query.shape[0]
    serve_count = serve_table.shape[0]
    long_count = long_request.shape[0]
    seq_index = lax.axis_index(SEQ)
    y_count = lax.axis_size("y")
    near_count = lax.axis_size("x") * lax.axis_size("c")
    seq_count = y_count * near_count
    tp_count = lax.axis_size("z")
    all_queries = lax.all_to_all(
        jnp.broadcast_to(query[None], (seq_count,) + query.shape), SEQ, 0, 0, tiled=True
    )
    all_queries = all_queries.reshape(-1, 2 * DH)
    total = seq_count * req_count
    pool_count = key_pool.shape[0]
    cell_count = key_pool.shape[1]
    long_cells = long_key.shape[1]
    groups = 16
    width = 2 * DV + 128
    safe_slot = jnp.maximum(page_slot, 0)
    cell_pos = page_offset[:, None] + jnp.arange(cell_count)[None, :]
    live = (page_slot[:, None] >= 0) & (cell_pos < serve_len[safe_slot][:, None])
    pool_group = jnp.where(live, page_slot[:, None], -1).reshape(1, -1)
    long_pos = seq_index * long_cells + jnp.arange(long_cells)
    long_live = long_pos[None, :] < long_len[:, None]
    long_group = jnp.where(long_live, serve_count + jnp.arange(long_count)[:, None], -1).reshape(1, -1)
    row_req = jnp.concatenate([serve_table, long_request], axis=0)
    row_req = jnp.concatenate([row_req, jnp.full((groups - row_req.shape[0],), -1, row_req.dtype)])
    outbox = outbox_kernel(
        row_req.reshape(groups, 1).astype(jnp.int32),
        all_queries,
        key_pool.reshape(pool_count * cell_count, -1),
        value_pool.reshape(pool_count * cell_count, -1),
        long_key.reshape(long_count * long_cells, -1),
        long_value.reshape(long_count * long_cells, -1),
        pool_group.astype(jnp.int32),
        long_group.astype(jnp.int32),
        near_count,
        req_count,
        width,
    )
    hop = lax.all_to_all(outbox.reshape(near_count, groups, width), ("x", "c"), 0, 0, tiled=True)
    hop = hop.reshape(near_count * groups, width).astype(jnp.float32)
    hop_num = hop[:, : 2 * DV].reshape(-1, 2, DV)
    hop_stats = join_three(hop[:, 2 * DV : 2 * DV + 12])
    hop_req = (hop[:, 2 * DV + 12] + hop[:, 2 * DV + 13]).astype(jnp.int32)
    merged_rows = y_count * req_count
    merged_at = (hop_req // (near_count * req_count)) * req_count + hop_req % req_count
    member = (hop_req[None, :] >= 0) & (merged_at[None, :] == jnp.arange(merged_rows)[:, None])
    member = member[:, :, None]
    hop_max = hop_stats[:, 0:2]
    merged_max = jnp.max(jnp.where(member, hop_max[None], MASKED), axis=1)
    scale = jnp.where(member, jnp.exp(jnp.where(member, hop_max[None] - merged_max[:, None], 0.0)), 0.0)
    merged_sum = jnp.einsum("tkj,kj->tj", scale, hop_stats[:, 2:4], precision=lax.Precision.HIGHEST)
    merged_num = jnp.einsum("tkj,kjv->tjv", scale, hop_num, precision=lax.Precision.HIGHEST)
    pieces = split_three(jnp.concatenate([merged_max, merged_sum], axis=1))
    spread = (jnp.arange(pieces.shape[1])[:, None] == jnp.arange(width - 2 * DV)[None, :])
    block = jnp.dot(pieces, spread.astype(jnp.bfloat16), preferred_element_type=jnp.float32)
    second = jnp.concatenate(
        [merged_num.reshape(merged_rows, 2 * DV).astype(jnp.bfloat16), block.astype(jnp.bfloat16)],
        axis=1,
    )
    inbox = lax.all_to_all(
        second.reshape(y_count, req_count, width), "y", 0, 0, tiled=True
    )
    sources = inbox.shape[0]
    in_num = inbox[:, :, : 2 * DV].astype(jnp.float32).reshape(sources, req_count, 2, DV)
    in_stats = join_three(inbox[:, :, 2 * DV : 2 * DV + 12])
    in_max = in_stats[:, :, 0:2]
    in_sum = in_stats[:, :, 2:4]
    own_queries = query.reshape(req_count, 2, DH)
    own_keys = new_key.reshape(req_count, 2, DH)
    own_scores = jnp.einsum(
        "rjd,rjd->rj", own_queries, own_keys, preferred_element_type=jnp.float32
    ) * DH ** (-0.5)
    best = jnp.maximum(own_scores, jnp.max(in_max, axis=0))
    factor = jnp.exp(in_max - best[None])
    own_weight = jnp.exp(own_scores - best)
    denom = own_weight + jnp.sum(factor * in_sum, axis=0)
    numer = own_weight[..., None] * new_value.reshape(req_count, 1, DV).astype(jnp.float32)
    numer = numer + jnp.sum(factor[..., None] * in_num, axis=0)
    attn = numer / denom[..., None]
    diff = attn[:, 0] - lambda_head[0] * attn[:, 1]
    normed = (
        diff
        * lax.rsqrt(jnp.mean(diff * diff, axis=-1, keepdims=True) + 1e-05)
        * norm_gain.reshape(1, DV)
    )
    normed = normed.astype(jnp.bfloat16)
    partial_out = jnp.dot(normed, out_weight, preferred_element_type=jnp.float32)
    cols = partial_out.shape[1] // tp_count
    pieces = lax.all_to_all(
        partial_out.reshape(req_count, tp_count, cols).transpose(1, 0, 2), "z", 0, 0, tiled=True
    )
    return jnp.sum(pieces, axis=0).astype(jnp.bfloat16)


SEQ = ("y", "x", "c")


def solution(mesh):
    y_count = mesh.shape["seq"] // 8
    parts = Mesh(mesh.devices.reshape(y_count, 4, 2, mesh.shape["tp"]), ("y", "x", "c", "z"))
    rows = P(SEQ, "z")
    pages = P(SEQ, None, "z")
    return jax.shard_map(
        on_device,
        mesh=parts,
        in_specs=(
            rows,
            rows,
            rows,
            pages,
            pages,
            P(None, SEQ, "z"),
            P(None, SEQ, "z"),
            P(SEQ),
            P(SEQ),
            P(SEQ),
            P(SEQ),
            P(),
            P(),
            P("z"),
            P("z"),
            P("z", None),
        ),
        out_specs=rows,
        check_vma=False,
    )
```

```python
import jax
import jax.numpy as jnp
from jax import lax
import functools

from jax.experimental import pallas as pl
from jax.sharding import Mesh, PartitionSpec as P

DH = 128
DV = 256
PG = 64


MASKED = -1e30


def _outbox_kernel(rr_ref, q_ref, kp_ref, vp_ref, lk_ref, lv_ref, colp_ref, coll_ref,
                   out_ref, *, groups, req_shift, near):
    rr = rr_ref[...]
    rr2 = jnp.concatenate([rr, rr], axis=0)
    total = q_ref.shape[0]
    qlane = lax.broadcasted_iota(jnp.int32, (2 * groups, total), 1)
    pick = (qlane == jnp.maximum(rr2, 0)).astype(jnp.bfloat16)
    qg = jnp.dot(pick, q_ref[...], preferred_element_type=jnp.float32)
    row = lax.broadcasted_iota(jnp.int32, qg.shape, 0)
    lane = lax.broadcasted_iota(jnp.int32, qg.shape, 1)
    keep = (lane < DH) == (row < groups)
    qsel = jnp.where(keep, qg, 0.0).astype(jnp.bfloat16)
    dims = (((1,), (1,)), ((), ()))
    s_pool = lax.dot_general(qsel, kp_ref[...], dims, preferred_element_type=jnp.float32) * DH ** (-0.5)
    s_long = lax.dot_general(qsel, lk_ref[...], dims, preferred_element_type=jnp.float32) * DH ** (-0.5)
    own = lax.broadcasted_iota(jnp.int32, (2 * groups, 1), 0)
    own = jnp.where(own < groups, own, own - groups)
    mask_pool = own == colp_ref[...]
    mask_long = own == coll_ref[...]
    s_pool = jnp.where(mask_pool, s_pool, MASKED)
    s_long = jnp.where(mask_long, s_long, MASKED)
    m = jnp.maximum(jnp.max(s_pool, axis=1, keepdims=True), jnp.max(s_long, axis=1, keepdims=True))
    w_pool = jnp.where(mask_pool, jnp.exp(s_pool - m), 0.0)
    w_long = jnp.where(mask_long, jnp.exp(s_long - m), 0.0)
    total = jnp.sum(w_pool, axis=1, keepdims=True) + jnp.sum(w_long, axis=1, keepdims=True)
    num = jnp.dot(w_pool.astype(jnp.bfloat16), vp_ref[...], preferred_element_type=jnp.float32)
    num = num + jnp.dot(w_long.astype(jnp.bfloat16), lv_ref[...], preferred_element_type=jnp.float32)
    numb = num.astype(jnp.bfloat16)
    stats = (m[:groups], m[groups:], total[:groups], total[groups:])
    slane = lax.broadcasted_iota(jnp.int32, (groups, 128), 1)
    id_hi = lax.shift_left(lax.shift_right_arithmetic(rr, 5), 5)
    id_lo = rr - id_hi
    block = jnp.where(
        slane == 12, id_hi.astype(jnp.float32), jnp.where(slane == 13, id_lo.astype(jnp.float32), 0.0)
    )
    for k, x in enumerate(stats):
        hi = x.astype(jnp.bfloat16).astype(jnp.float32)
        rest = x - hi
        mid = rest.astype(jnp.bfloat16).astype(jnp.float32)
        lo = rest - mid
        for piece, value in enumerate((hi, mid, lo)):
            block = jnp.where(slane == piece * 4 + k, value, block)
    packed = jnp.concatenate(
        [numb[:groups], numb[groups:], block.astype(jnp.bfloat16)], axis=1
    )
    rrb = jnp.concatenate([rr] * near, axis=0)
    prow = lax.broadcasted_iota(jnp.int32, rrb.shape, 0)
    slot = prow % groups
    dest = jnp.where(rrb >= 0, lax.shift_right_logical(rrb, req_shift) % near, -1)
    hit = dest == prow // groups
    glane = lax.broadcasted_iota(jnp.int32, (near * groups, groups), 1)
    place = ((glane == slot) & hit) | ((glane == groups - 1) & jnp.logical_not(hit))
    out_ref[...] = jnp.dot(
        place.astype(jnp.bfloat16), packed, preferred_element_type=jnp.float32
    ).astype(out_ref.dtype)


def outbox_kernel(rr, q_all, kp, vp, lk, lv, colp, coll, near, req_count, width, interpret=False):
    groups = rr.shape[0]
    req_shift = req_count.bit_length() - 1
    assert req_count == 1 << req_shift
    kern = functools.partial(_outbox_kernel, groups=groups, req_shift=req_shift, near=near)
    return pl.pallas_call(
        kern,
        out_shape=jax.ShapeDtypeStruct((near * groups, width), jnp.bfloat16),
        interpret=interpret,
    )(rr, q_all, kp, vp, lk, lv, colp, coll)


def split_three(x):
    hi = lax.reduce_precision(x, exponent_bits=8, mantissa_bits=7)
    rest = x - hi
    mid = lax.reduce_precision(rest, exponent_bits=8, mantissa_bits=7)
    lo = rest - mid
    return jnp.concatenate([hi, mid, lo], axis=-1).astype(jnp.bfloat16)


def join_three(x):
    n = x.shape[-1] // 3
    x = x.astype(jnp.float32)
    return (x[..., :n] + x[..., n : 2 * n]) + x[..., 2 * n :]


def on_device(
    query,
    new_key,
    new_value,
    key_pool,
    value_pool,
    long_key,
    long_value,
    serve_table,
    serve_len,
    page_slot,
    page_offset,
    long_request,
    long_len,
    lambda_head,
    norm_gain,
    out_weight,
):
    req_count = query.shape[0]
    serve_count = serve_table.shape[0]
    long_count = long_request.shape[0]
    seq_index = lax.axis_index(SEQ)
    y_count = lax.axis_size("y")
    near_count = lax.axis_size("x") * lax.axis_size("c")
    seq_count = y_count * near_count
    tp_count = lax.axis_size("z")
    all_queries = lax.all_to_all(
        jnp.broadcast_to(query[None], (seq_count,) + query.shape), SEQ, 0, 0, tiled=True
    )
    all_queries = all_queries.reshape(-1, 2 * DH)
    total = seq_count * req_count
    pool_count = key_pool.shape[0]
    cell_count = key_pool.shape[1]
    long_cells = long_key.shape[1]
    groups = 16
    width = 2 * DV + 128
    safe_slot = jnp.maximum(page_slot, 0)
    cell_pos = page_offset[:, None] + jnp.arange(cell_count)[None, :]
    live = (page_slot[:, None] >= 0) & (cell_pos < serve_len[safe_slot][:, None])
    pool_group = jnp.where(live, page_slot[:, None], -1).reshape(1, -1)
    long_pos = seq_index * long_cells + jnp.arange(long_cells)
    long_live = long_pos[None, :] < long_len[:, None]
    long_group = jnp.where(long_live, serve_count + jnp.arange(long_count)[:, None], -1).reshape(1, -1)
    row_req = jnp.concatenate([serve_table, long_request], axis=0)
    row_req = jnp.concatenate([row_req, jnp.full((groups - row_req.shape[0],), -1, row_req.dtype)])
    outbox = outbox_kernel(
        row_req.reshape(groups, 1).astype(jnp.int32),
        all_queries,
        key_pool.reshape(pool_count * cell_count, -1),
        value_pool.reshape(pool_count * cell_count, -1),
        long_key.reshape(long_count * long_cells, -1),
        long_value.reshape(long_count * long_cells, -1),
        pool_group.astype(jnp.int32),
        long_group.astype(jnp.int32),
        near_count,
        req_count,
        width,
    )
    hop = lax.all_to_all(outbox.reshape(near_count, groups, width), ("x", "c"), 0, 0, tiled=True)
    hop = hop.reshape(near_count * groups, width).astype(jnp.float32)
    hop_num = hop[:, : 2 * DV].reshape(-1, 2, DV)
    hop_stats = join_three(hop[:, 2 * DV : 2 * DV + 12])
    hop_req = (hop[:, 2 * DV + 12] + hop[:, 2 * DV + 13]).astype(jnp.int32)
    merged_rows = y_count * req_count
    merged_at = (hop_req // (near_count * req_count)) * req_count + hop_req % req_count
    member = (hop_req[None, :] >= 0) & (merged_at[None, :] == jnp.arange(merged_rows)[:, None])
    member = member[:, :, None]
    hop_max = hop_stats[:, 0:2]
    merged_max = jnp.max(jnp.where(member, hop_max[None], MASKED), axis=1)
    scale = jnp.where(member, jnp.exp(jnp.where(member, hop_max[None] - merged_max[:, None], 0.0)), 0.0)
    merged_sum = jnp.einsum("tkj,kj->tj", scale, hop_stats[:, 2:4], precision=lax.Precision.HIGHEST)
    merged_num = jnp.einsum("tkj,kjv->tjv", scale, hop_num, precision=lax.Precision.HIGHEST)
    pieces = split_three(jnp.concatenate([merged_max, merged_sum], axis=1))
    spread = (jnp.arange(pieces.shape[1])[:, None] == jnp.arange(width - 2 * DV)[None, :])
    block = jnp.dot(pieces, spread.astype(jnp.bfloat16), preferred_element_type=jnp.float32)
    second = jnp.concatenate(
        [merged_num.reshape(merged_rows, 2 * DV).astype(jnp.bfloat16), block.astype(jnp.bfloat16)],
        axis=1,
    )
    inbox = lax.all_to_all(
        second.reshape(y_count, req_count, width), "y", 0, 0, tiled=True
    )
    sources = inbox.shape[0]
    in_num = inbox[:, :, : 2 * DV].astype(jnp.float32).reshape(sources, req_count, 2, DV)
    in_stats = join_three(inbox[:, :, 2 * DV : 2 * DV + 12])
    in_max = in_stats[:, :, 0:2]
    in_sum = in_stats[:, :, 2:4]
    own_queries = query.reshape(req_count, 2, DH)
    own_keys = new_key.reshape(req_count, 2, DH)
    own_scores = jnp.einsum(
        "rjd,rjd->rj", own_queries, own_keys, preferred_element_type=jnp.float32
    ) * DH ** (-0.5)
    best = jnp.maximum(own_scores, jnp.max(in_max, axis=0))
    factor = jnp.exp(in_max - best[None])
    own_weight = jnp.exp(own_scores - best)
    denom = own_weight + jnp.sum(factor * in_sum, axis=0)
    numer = own_weight[..., None] * new_value.reshape(req_count, 1, DV).astype(jnp.float32)
    numer = numer + jnp.sum(factor[..., None] * in_num, axis=0)
    attn = numer / denom[..., None]
    diff = attn[:, 0] - lambda_head[0] * attn[:, 1]
    normed = (
        diff
        * lax.rsqrt(jnp.mean(diff * diff, axis=-1, keepdims=True) + 1e-05)
        * norm_gain.reshape(1, DV)
    )
    normed = normed.astype(jnp.bfloat16)
    partial_out = jnp.dot(normed, out_weight, preferred_element_type=jnp.float32)
    cols = partial_out.shape[1] // tp_count
    pieces = lax.all_to_all(
        partial_out.astype(jnp.bfloat16).reshape(req_count, tp_count, cols).transpose(1, 0, 2), "z", 0, 0, tiled=True
    )
    return jnp.sum(pieces.astype(jnp.float32), axis=0).astype(jnp.bfloat16)


SEQ = ("y", "x", "c")


def solution(mesh):
    y_count = mesh.shape["seq"] // 8
    parts = Mesh(mesh.devices.reshape(y_count, 4, 2, mesh.shape["tp"]), ("y", "x", "c", "z"))
    rows = P(SEQ, "z")
    pages = P(SEQ, None, "z")
    return jax.shard_map(
        on_device,
        mesh=parts,
        in_specs=(
            rows,
            rows,
            rows,
            pages,
            pages,
            P(None, SEQ, "z"),
            P(None, SEQ, "z"),
            P(SEQ),
            P(SEQ),
            P(SEQ),
            P(SEQ),
            P(),
            P(),
            P("z"),
            P("z"),
            P("z", None),
        ),
        out_specs=rows,
        check_vma=False,
    )
```

```python
import jax
import jax.numpy as jnp
from jax import lax
import functools

from jax.experimental import pallas as pl
from jax.sharding import Mesh, PartitionSpec as P

DH = 128
DV = 256
PG = 64


MASKED = -1e30


def _outbox_kernel(rr_ref, q_ref, kp_ref, vp_ref, lk_ref, lv_ref, colp_ref, coll_ref,
                   out_ref, *, groups, req_shift, near):
    rr = rr_ref[...]
    rr2 = jnp.concatenate([rr, rr], axis=0)
    total = q_ref.shape[0]
    qlane = lax.broadcasted_iota(jnp.int32, (2 * groups, total), 1)
    pick = (qlane == jnp.maximum(rr2, 0)).astype(jnp.bfloat16)
    qg = jnp.dot(pick, q_ref[...], preferred_element_type=jnp.float32)
    row = lax.broadcasted_iota(jnp.int32, qg.shape, 0)
    lane = lax.broadcasted_iota(jnp.int32, qg.shape, 1)
    keep = (lane < DH) == (row < groups)
    qsel = jnp.where(keep, qg, 0.0).astype(jnp.bfloat16)
    dims = (((1,), (1,)), ((), ()))
    s_pool = lax.dot_general(qsel, kp_ref[...], dims, preferred_element_type=jnp.float32) * DH ** (-0.5)
    s_long = lax.dot_general(qsel, lk_ref[...], dims, preferred_element_type=jnp.float32) * DH ** (-0.5)
    own = lax.broadcasted_iota(jnp.int32, (2 * groups, 1), 0)
    own = jnp.where(own < groups, own, own - groups)
    mask_pool = own == colp_ref[...]
    mask_long = own == coll_ref[...]
    s_pool = jnp.where(mask_pool, s_pool, MASKED)
    s_long = jnp.where(mask_long, s_long, MASKED)
    m = jnp.maximum(jnp.max(s_pool, axis=1, keepdims=True), jnp.max(s_long, axis=1, keepdims=True))
    w_pool = jnp.where(mask_pool, jnp.exp(s_pool - m), 0.0)
    w_long = jnp.where(mask_long, jnp.exp(s_long - m), 0.0)
    total = jnp.sum(w_pool, axis=1, keepdims=True) + jnp.sum(w_long, axis=1, keepdims=True)
    num = jnp.dot(w_pool.astype(jnp.bfloat16), vp_ref[...], preferred_element_type=jnp.float32)
    num = num + jnp.dot(w_long.astype(jnp.bfloat16), lv_ref[...], preferred_element_type=jnp.float32)
    numb = num.astype(jnp.bfloat16)
    stats = (m[:groups], m[groups:], total[:groups], total[groups:])
    slane = lax.broadcasted_iota(jnp.int32, (groups, 128), 1)
    id_hi = lax.shift_left(lax.shift_right_arithmetic(rr, 5), 5)
    id_lo = rr - id_hi
    block = jnp.where(
        slane == 12, id_hi.astype(jnp.float32), jnp.where(slane == 13, id_lo.astype(jnp.float32), 0.0)
    )
    for k, x in enumerate(stats):
        hi = x.astype(jnp.bfloat16).astype(jnp.float32)
        rest = x - hi
        mid = rest.astype(jnp.bfloat16).astype(jnp.float32)
        lo = rest - mid
        for piece, value in enumerate((hi, mid, lo)):
            block = jnp.where(slane == piece * 4 + k, value, block)
    packed = jnp.concatenate(
        [numb[:groups], numb[groups:], block.astype(jnp.bfloat16)], axis=1
    )
    rrb = jnp.concatenate([rr] * near, axis=0)
    prow = lax.broadcasted_iota(jnp.int32, rrb.shape, 0)
    slot = prow % groups
    dest = jnp.where(rrb >= 0, lax.shift_right_logical(rrb, req_shift) % near, -1)
    hit = dest == prow // groups
    glane = lax.broadcasted_iota(jnp.int32, (near * groups, groups), 1)
    place = ((glane == slot) & hit) | ((glane == groups - 1) & jnp.logical_not(hit))
    out_ref[...] = jnp.dot(
        place.astype(jnp.bfloat16), packed, preferred_element_type=jnp.float32
    ).astype(out_ref.dtype)


def outbox_kernel(rr, q_all, kp, vp, lk, lv, colp, coll, near, req_count, width, interpret=False):
    groups = rr.shape[0]
    req_shift = req_count.bit_length() - 1
    assert req_count == 1 << req_shift
    kern = functools.partial(_outbox_kernel, groups=groups, req_shift=req_shift, near=near)
    return pl.pallas_call(
        kern,
        out_shape=jax.ShapeDtypeStruct((near * groups, width), jnp.bfloat16),
        interpret=interpret,
    )(rr, q_all, kp, vp, lk, lv, colp, coll)


def split_three(x):
    hi = lax.reduce_precision(x, exponent_bits=8, mantissa_bits=7)
    rest = x - hi
    mid = lax.reduce_precision(rest, exponent_bits=8, mantissa_bits=7)
    lo = rest - mid
    return jnp.concatenate([hi, mid, lo], axis=-1).astype(jnp.bfloat16)


def join_three(x):
    n = x.shape[-1] // 3
    x = x.astype(jnp.float32)
    return (x[..., :n] + x[..., n : 2 * n]) + x[..., 2 * n :]


def on_device(
    query,
    new_key,
    new_value,
    key_pool,
    value_pool,
    long_key,
    long_value,
    serve_table,
    serve_len,
    page_slot,
    page_offset,
    long_request,
    long_len,
    lambda_head,
    norm_gain,
    out_weight,
):
    req_count = query.shape[0]
    serve_count = serve_table.shape[0]
    long_count = long_request.shape[0]
    seq_index = lax.axis_index(SEQ)
    y_count = lax.axis_size("y")
    near_count = lax.axis_size("x") * lax.axis_size("c")
    seq_count = y_count * near_count
    tp_count = lax.axis_size("z")
    all_queries = lax.all_to_all(
        jnp.broadcast_to(query[None], (seq_count,) + query.shape), SEQ, 0, 0, tiled=True
    )
    all_queries = all_queries.reshape(-1, 2 * DH)
    total = seq_count * req_count
    pool_count = key_pool.shape[0]
    cell_count = key_pool.shape[1]
    long_cells = long_key.shape[1]
    groups = 16
    width = 2 * DV + 128
    safe_slot = jnp.maximum(page_slot, 0)
    cell_pos = page_offset[:, None] + jnp.arange(cell_count)[None, :]
    live = (page_slot[:, None] >= 0) & (cell_pos < serve_len[safe_slot][:, None])
    pool_group = jnp.where(live, page_slot[:, None], -1).reshape(1, -1)
    long_pos = seq_index * long_cells + jnp.arange(long_cells)
    long_live = long_pos[None, :] < long_len[:, None]
    long_group = jnp.where(long_live, serve_count + jnp.arange(long_count)[:, None], -1).reshape(1, -1)
    row_req = jnp.concatenate([serve_table, long_request], axis=0)
    row_req = jnp.concatenate([row_req, jnp.full((groups - row_req.shape[0],), -1, row_req.dtype)])
    outbox = outbox_kernel(
        row_req.reshape(groups, 1).astype(jnp.int32),
        all_queries,
        key_pool.reshape(pool_count * cell_count, -1),
        value_pool.reshape(pool_count * cell_count, -1),
        long_key.reshape(long_count * long_cells, -1),
        long_value.reshape(long_count * long_cells, -1),
        pool_group.astype(jnp.int32),
        long_group.astype(jnp.int32),
        near_count,
        req_count,
        width,
    )
    hop = lax.all_to_all(outbox.reshape(near_count, groups, width), ("x", "c"), 0, 0, tiled=True)
    hop = hop.reshape(near_count * groups, width).astype(jnp.float32)
    hop_num = hop[:, : 2 * DV].reshape(-1, 2, DV)
    hop_stats = join_three(hop[:, 2 * DV : 2 * DV + 12])
    hop_req = (hop[:, 2 * DV + 12] + hop[:, 2 * DV + 13]).astype(jnp.int32)
    merged_rows = y_count * req_count
    merged_at = (hop_req // (near_count * req_count)) * req_count + hop_req % req_count
    member = (hop_req[None, :] >= 0) & (merged_at[None, :] == jnp.arange(merged_rows)[:, None])
    member = member[:, :, None]
    hop_max = hop_stats[:, 0:2]
    merged_max = jnp.max(jnp.where(member, hop_max[None], MASKED), axis=1)
    scale = jnp.where(member, jnp.exp(jnp.where(member, hop_max[None] - merged_max[:, None], 0.0)), 0.0)
    merged_sum = jnp.einsum("tkj,kj->tj", scale, hop_stats[:, 2:4], precision=lax.Precision.HIGHEST)
    merged_num = jnp.einsum("tkj,kjv->tjv", scale, hop_num, preferred_element_type=jnp.float32)
    pieces = split_three(jnp.concatenate([merged_max, merged_sum], axis=1))
    spread = (jnp.arange(pieces.shape[1])[:, None] == jnp.arange(width - 2 * DV)[None, :])
    block = jnp.dot(pieces, spread.astype(jnp.bfloat16), preferred_element_type=jnp.float32)
    second = jnp.concatenate(
        [merged_num.reshape(merged_rows, 2 * DV).astype(jnp.bfloat16), block.astype(jnp.bfloat16)],
        axis=1,
    )
    inbox = lax.all_to_all(
        second.reshape(y_count, req_count, width), "y", 0, 0, tiled=True
    )
    sources = inbox.shape[0]
    in_num = inbox[:, :, : 2 * DV].astype(jnp.float32).reshape(sources, req_count, 2, DV)
    in_stats = join_three(inbox[:, :, 2 * DV : 2 * DV + 12])
    in_max = in_stats[:, :, 0:2]
    in_sum = in_stats[:, :, 2:4]
    own_queries = query.reshape(req_count, 2, DH)
    own_keys = new_key.reshape(req_count, 2, DH)
    own_scores = jnp.einsum(
        "rjd,rjd->rj", own_queries, own_keys, preferred_element_type=jnp.float32
    ) * DH ** (-0.5)
    best = jnp.maximum(own_scores, jnp.max(in_max, axis=0))
    factor = jnp.exp(in_max - best[None])
    own_weight = jnp.exp(own_scores - best)
    denom = own_weight + jnp.sum(factor * in_sum, axis=0)
    numer = own_weight[..., None] * new_value.reshape(req_count, 1, DV).astype(jnp.float32)
    numer = numer + jnp.sum(factor[..., None] * in_num, axis=0)
    attn = numer / denom[..., None]
    diff = attn[:, 0] - lambda_head[0] * attn[:, 1]
    normed = (
        diff
        * lax.rsqrt(jnp.mean(diff * diff, axis=-1, keepdims=True) + 1e-05)
        * norm_gain.reshape(1, DV)
    )
    normed = normed.astype(jnp.bfloat16)
    partial_out = jnp.dot(normed, out_weight, preferred_element_type=jnp.float32)
    cols = partial_out.shape[1] // tp_count
    pieces = lax.all_to_all(
        partial_out.astype(jnp.bfloat16).reshape(req_count, tp_count, cols).transpose(1, 0, 2), "z", 0, 0, tiled=True
    )
    return jnp.sum(pieces.astype(jnp.float32), axis=0).astype(jnp.bfloat16)


SEQ = ("y", "x", "c")


def solution(mesh):
    y_count = mesh.shape["seq"] // 8
    parts = Mesh(mesh.devices.reshape(y_count, 4, 2, mesh.shape["tp"]), ("y", "x", "c", "z"))
    rows = P(SEQ, "z")
    pages = P(SEQ, None, "z")
    return jax.shard_map(
        on_device,
        mesh=parts,
        in_specs=(
            rows,
            rows,
            rows,
            pages,
            pages,
            P(None, SEQ, "z"),
            P(None, SEQ, "z"),
            P(SEQ),
            P(SEQ),
            P(SEQ),
            P(SEQ),
            P(),
            P(),
            P("z"),
            P("z"),
            P("z", None),
        ),
        out_specs=rows,
        check_vma=False,
    )
```
